32 devices in a mesh: parts: 2 (over y), tile: 4 (over z), depth: 2 (over x), sub: 2 (over core).
Axes of the slice: x: 2, y: 2, z: 4, core: 2. Of those that a mesh axis runs over, the one named last changes fastest.
Arguments:
- left_mantissa: bfloat16 [512, 512], P(('parts', 'depth'), 'tile'), parts along dimension 0, may hold values from -6 to 6
- left_exponent: int32 [512, 16], P(('parts', 'depth'), 'tile'), parts along dimension 0, may hold values from -2 to 1
- right_mantissa: bfloat16 [512, 512], P(('parts', 'depth'), ('tile', 'sub')), parts along dimension 0, may hold values from -6 to 6
- right_exponent: int32 [512, 16], P(('parts', 'depth'), ('tile', 'sub')), parts along dimension 0, may hold values from -2 to 1
- residue_mask: int32 [32], P('parts'), parts along dimension 0, may hold values 0 or 1
- out_weight: bfloat16 [1024, 128], replicated, may hold values from -3 to 3
- out_bias: float32 [128], replicated, may hold values from -3 to 3
- gate_weight: bfloat16 [128, 512], replicated, may hold values from -0.5 to 0.5
- up_weight: bfloat16 [128, 512], replicated, may hold values from -0.5 to 0.5
- down_weight: bfloat16 [512, 128], replicated, may hold values from -0.25 to 0.25
- distogram_weight: bfloat16 [128, 64], replicated, may hold values from -0.5 to 0.5
- distogram_bias: float32 [64], replicated, may hold values from -3 to 3
Outputs:
- symmetric_pair: bfloat16 [32, 2048], P(('parts', 'tile', 'depth', 'sub')), parts along dimension 0
- distogram: float32 [32, 1024], P(('parts', 'tile', 'depth', 'sub')), parts along dimension 0
The draws below stay inside these ranges and needn't reach their ends.
There are 2 independent parts, one for each index of `parts`. The reference program is written for one: setup_inputs(seed, part) draws one part's arguments, and reference() takes and returns one part's arrays. A program takes and returns all parts, laid end to end along the dimension named above; an argument that names none is the same for every part. Nothing has to cross between parts.
All inputs are finite; a program needn't handle non-finite values.
Results may differ from the reference program's by a relative error of at most 0.007.
Values may be sent and summed in bfloat16 or wider, within the bound.
No kernel may reach another device: no remote copies, remote signals or barrier semaphores. Data moves between devices by JAX's collectives and lax.ppermute only.
A program may use at most 64 MiB of HBM per device.

```python
import math
import jax
import jax.numpy as jnp
from jax import lax

C = 32
PC = 128
HID = 512
BINS = 64
SEQS = 256
RES = 16


def place_ends(result, rng, smallest, high):
    longest = result.shape.index(max(result.shape))
    spots = []
    for shift in (0, 1):
        where = [jax.random.randint(jax.random.fold_in(rng, axis), (), 0, length) for axis, length in enumerate(result.shape)]
        where[longest] = (where[longest] + shift) % result.shape[longest]
        spots.append(tuple(where))
    return result.at[spots[0]].set(smallest).at[spots[1]].set(high)


def levels(stream_key, extent, cuts, smallest, largest):
    def one(dim, shards_of):
        heights = jax.random.uniform(jax.random.fold_in(jax.random.fold_in(stream_key, 6), dim), (shards_of,), jnp.float32, smallest / len(cuts), largest / len(cuts))
        return jnp.repeat(jnp.exp(heights), extent[dim] // shards_of).reshape((-1,) + (1,) * (len(extent) - dim - 1))

    loudness = one(*cuts[0])
    for cut in cuts[1:]:
        loudness = loudness * one(*cut)
    return loudness


def bell_draw(own_key, dims, scale, reach, split=(), kind=jnp.bfloat16):
    loudness = levels(own_key, dims, split, -0.22, 0.18) if split else 1.0
    drawn = jax.random.normal(own_key, dims, jnp.float32) * scale * loudness
    return jnp.minimum(jnp.maximum(drawn, -reach), reach).astype(kind)


def setup_inputs(seed: int = 0, part: int = 0) -> dict:
    seeds = jax.random.split(jax.random.key(seed), 13)
    part_keys = jax.random.split(jax.random.fold_in(seeds[12], part), 13)
    left_mantissa = bell_draw(part_keys[0], (SEQS, RES * C), 1.0, 6.0, ((0, 2), (1, 4)))
    left_exponent = place_ends(jax.random.randint(part_keys[1], (SEQS, RES), -2, 2), jax.random.fold_in(part_keys[1], 1), -2, 1).astype(jnp.int32)
    right_mantissa = bell_draw(part_keys[2], (SEQS, RES * C), 1.0, 6.0, ((0, 2), (1, 8)))
    right_exponent = place_ends(jax.random.randint(part_keys[3], (SEQS, RES), -2, 2), jax.random.fold_in(part_keys[3], 1), -2, 1).astype(jnp.int32)
    residue_mask = place_ends((jax.random.randint(part_keys[4], (RES,), 0, 4) < 3).astype(jnp.int32), jax.random.fold_in(part_keys[4], 1), 0, 1)
    out_weight = bell_draw(seeds[5], (C * C, PC), 0.5, 3.0)
    out_bias = bell_draw(seeds[6], (PC,), 0.5, 3.0, (), jnp.float32)
    gate_weight = bell_draw(seeds[7], (PC, HID), PC ** -0.5, 0.5)
    up_weight = bell_draw(seeds[8], (PC, HID), PC ** -0.5, 0.5)
    down_weight = bell_draw(seeds[9], (HID, PC), HID ** -0.5, 0.25)
    distogram_weight = bell_draw(seeds[10], (PC, BINS), PC ** -0.5, 0.5)
    distogram_bias = bell_draw(seeds[11], (BINS,), 0.5, 3.0, (), jnp.float32)
    return {"left_mantissa": left_mantissa, "left_exponent": left_exponent, "right_mantissa": right_mantissa, "right_exponent": right_exponent, "residue_mask": residue_mask, "out_weight": out_weight, "out_bias": out_bias, "gate_weight": gate_weight, "up_weight": up_weight, "down_weight": down_weight, "distogram_weight": distogram_weight, "distogram_bias": distogram_bias}


def dequantize(mantissa, exponent, keep_mask):
    seq_count, columns = mantissa.shape
    residues = exponent.shape[1]
    channels = columns // residues
    scaling = jnp.exp2(exponent.astype(jnp.float32))[:, :, None] * keep_mask.astype(jnp.float32)[None, :, None]
    values = mantissa.astype(jnp.float32).reshape(seq_count, residues, channels) * scaling
    return values.astype(jnp.bfloat16).reshape(seq_count, columns)

def transition(pair_rows, gate_weight, up_weight, down_weight):
    values = pair_rows.astype(jnp.float32)
    center = lax.optimization_barrier(jnp.mean(values, axis=-1, keepdims=True))
    spread = lax.optimization_barrier(jnp.mean((values - center) ** 2, axis=-1, keepdims=True))
    normed = ((values - center) * lax.rsqrt(spread + 1e-05)).astype(jnp.bfloat16)
    gate_part = jnp.dot(normed, gate_weight, preferred_element_type=jnp.float32)
    up_part = jnp.dot(normed, up_weight, preferred_element_type=jnp.float32)
    hidden = (jax.nn.silu(gate_part) * up_part).astype(jnp.bfloat16)
    return (values + jnp.dot(hidden, down_weight, preferred_element_type=jnp.float32)).astype(jnp.bfloat16)

def reference(left_mantissa, left_exponent, right_mantissa, right_exponent, residue_mask, out_weight, out_bias, gate_weight, up_weight, down_weight, distogram_weight, distogram_bias):
    left_full = dequantize(left_mantissa, left_exponent, residue_mask).astype(jnp.float32)
    right_full = dequantize(right_mantissa, right_exponent, residue_mask).astype(jnp.float32)
    projector = out_weight.astype(jnp.float32).reshape(C, C, PC)
    block_rows = math.gcd(RES, 8)

    def one_block(block_index):
        row_slice = lax.dynamic_slice_in_dim(left_full, block_index * (block_rows * C), block_rows * C, 1)
        outer = jnp.dot(row_slice.T, right_full, precision=lax.Precision.HIGHEST) / SEQS
        outer = outer.reshape(block_rows, C, RES, C)
        mixed = jnp.einsum('icje,cek->ijk', outer, projector, precision=lax.Precision.HIGHEST) + out_bias
        return transition(mixed.astype(jnp.bfloat16), gate_weight, up_weight, down_weight)
    moved = lax.map(one_block, jnp.arange(RES // block_rows, dtype=jnp.int32)).reshape(RES, RES, PC)
    moved_wide = moved.astype(jnp.float32)
    symmetric = ((moved_wide + jnp.transpose(moved_wide, (1, 0, 2))) * 0.5).astype(jnp.bfloat16)
    logits = jnp.dot(symmetric, distogram_weight, preferred_element_type=jnp.float32) + distogram_bias
    return (symmetric.reshape(RES, RES * PC), logits.reshape(RES, RES * BINS))
```

```python
import functools

import jax
import jax.numpy as jnp
from jax import lax
from jax.experimental import pallas as pl
from jax.experimental.pallas import tpu as pltpu
from jax.sharding import PartitionSpec as P


LANES = 128
ROWS = 8
GROUP = ("tile", "depth", "sub")
NT = (((1,), (1,)), ((), ()))
VMEM = pl.BlockSpec(memory_space=pltpu.VMEM)
SMEM = pl.BlockSpec(memory_space=pltpu.SMEM)


def parity(number):
    return bin(number).count("1") & 1


def xor_permute(value, tile_bits, depth_bits, sub_bits):
    depth_count, sub_count = lax.axis_size("depth"), lax.axis_size("sub")
    pairs = []
    for t in range(lax.axis_size("tile")):
        for d in range(depth_count):
            for s in range(sub_count):
                here = (t * depth_count + d) * sub_count + s
                there = ((t ^ tile_bits) * depth_count + (d ^ depth_bits)) * sub_count + (s ^ sub_bits)
                pairs.append((here, there))
    return lax.ppermute(value, GROUP, pairs)


def bits_of(count):
    return [1 << b for b in reversed(range(count.bit_length() - 1))]


def row_in_tile(sub_count):
    return lax.axis_index("depth") * sub_count + lax.axis_index("sub")


def prepare_kernel(
    dims, left_ref, left_exp_ref, right_ref, right_exp_ref, mask_ref, block_ref, left_out, right_out, left_f32
):
    channels, _, sub_count = dims
    band = left_exp_ref.shape[0]
    piece = right_exp_ref.shape[0]
    fold = channels // ROWS
    tile, sub = lax.axis_index("tile"), lax.axis_index("sub")
    mine = row_in_tile(sub_count)
    right = right_ref[...].astype(jnp.float32)
    right_scale = jnp.exp2(right_exp_ref[...].astype(jnp.float32))
    first = tile * band + sub * piece
    scaled = []
    for j in range(piece):
        scale = right_scale[j : j + 1] * mask_ref[first + j].astype(jnp.float32)
        scaled.append(right[j * channels : (j + 1) * channels] * scale)
        right_out[j * channels : (j + 1) * channels, :] = scaled[j].astype(jnp.bfloat16)
    half = fold * piece * ROWS
    for x in range(fold):
        rows = jnp.concatenate([scaled[j][x * ROWS : (x + 1) * ROWS] for j in range(piece)], axis=0)
        at = half + x * piece * ROWS
        block_ref[at : at + piece * ROWS, :] = rows.astype(jnp.bfloat16)
    left = jnp.transpose(left_ref[...].astype(jnp.float32))
    left_scale = jnp.exp2(left_exp_ref[...].astype(jnp.float32))
    for i in range(band):
        scale = left_scale[i : i + 1] * mask_ref[tile * band + i].astype(jnp.float32)
        left_f32[i * channels : (i + 1) * channels, :] = left[i * channels : (i + 1) * channels] * scale
    for x in range(fold):
        rows = []
        for j in range(piece):
            at = pl.multiple_of((sub * piece + j) * channels + x * ROWS, ROWS)
            rows.append(left_f32[pl.ds(at, ROWS), :])
        at = x * piece * ROWS
        block_ref[at : at + piece * ROWS, :] = jnp.concatenate(rows, axis=0).astype(jnp.bfloat16)
    for i in range(band):
        at = pl.multiple_of((mine ^ i) * channels, channels)
        left_out[i * channels : (i + 1) * channels, :] = left_f32[pl.ds(at, channels), :].astype(jnp.bfloat16)


def spread_kernel(
    dims, left_ref, right_ref, other_ref, weight_ref, left_spread, right_spread, weight_out, both, weight_f32
):
    channels, _, sub_count = dims
    seqs = left_ref.shape[1]
    band = left_ref.shape[0] // channels
    piece = right_ref.shape[0] // channels
    fold = channels // ROWS
    sub = lax.axis_index("sub")
    mine = row_in_tile(sub_count)
    both[sub] = right_ref[...].reshape(piece, channels, seqs)
    both[1 - sub] = other_ref[...].reshape(piece, channels, seqs)
    left_spread[...] = jnp.zeros_like(left_spread)
    right_spread[...] = jnp.zeros_like(right_spread)
    for i in range(band):
        here = mine ^ i
        left = left_ref[i * channels : (i + 1) * channels, :]
        right = both[here // piece, here % piece]
        for x in range(fold):
            at = (i * fold + x) * channels
            left_spread[at : at + channels, x * seqs : (x + 1) * seqs] = left
            right_spread[at : at + channels, x * seqs : (x + 1) * seqs] = right
    weight_f32[...] = weight_ref[...].astype(jnp.float32)
    for g in range(ROWS):
        for x in range(fold):
            at = (g * fold + x) * channels
            rows = weight_f32[pl.ds(x * ROWS + g, channels, stride=channels), :]
            weight_out[at : at + channels, :] = rows.astype(jnp.bfloat16)


def pair_kernel(dims, block_count, *refs):
    channels, _, sub_count = dims
    blocks = refs[:block_count]
    left_spread, right_spread, weight_ref, swapped_ref, keep_ref, core_ref, chip_ref, outer = refs[block_count:]
    fold = channels // ROWS
    half = blocks[0].shape[0] // 2
    size = half // fold
    piece = size // ROWS
    count = block_count * piece
    band = left_spread.shape[0] // (fold * channels)
    width = fold * channels
    natural = jnp.concatenate(
        [
            weight_ref[(x * ROWS + g) * channels : (x * ROWS + g + 1) * channels, :]
            for g in range(ROWS)
            for x in range(fold)
        ],
        axis=0,
    )
    for way in range(2):
        base = half * (1 - way)
        factor = jnp.concatenate(
            [
                jnp.concatenate([b[base + x * size : base + (x + 1) * size, :] for b in blocks], axis=0)
                for x in range(fold)
            ],
            axis=1,
        )
        spread = left_spread if way == 0 else right_spread
        product = lax.dot_general(factor, spread[...], NT, preferred_element_type=jnp.float32)
        for i in range(band):
            outer[way * band + i] = product[:, i * width : (i + 1) * width]
        flat = jnp.concatenate(
            [
                jnp.concatenate(
                    [outer[way * band + i, pl.ds(g, count, stride=ROWS), :] for g in range(ROWS)],
                    axis=1,
                )
                for i in range(band)
            ],
            axis=0,
        )
        high = flat.astype(jnp.bfloat16)
        low = (flat - high.astype(jnp.float32)).astype(jnp.bfloat16)
        weight = swapped_ref[...] if way == 0 else natural
        terms = jnp.dot(jnp.concatenate([high, low], axis=0), weight, preferred_element_type=jnp.float32)
        terms = terms[: band * count] + terms[band * count :]
        place = lambda i: slice(i * count, (i + 1) * count)
        keep_ref[place(way), :] = terms[place(0)]
        core_ref[place(way), :] = terms[place(1)]
        for i in range(sub_count, band):
            chip_ref[place((i - sub_count) * 2 + way), :] = terms[place(i)]


def finish_kernel(
    dims,
    block_tiles,
    total_seqs,
    keep_ref,
    core_ref,
    chip_ref,
    relay_ref,
    out_bias,
    gate_weight,
    up_weight,
    down_weight,
    bins_weight,
    bins_bias,
    symmetric_out,
    bins_out,
):
    _, depth_count, sub_count = dims
    pair_channels = gate_weight.shape[0]
    bins = bins_weight.shape[0]
    count = keep_ref.shape[0] // 2
    piece = count // len(block_tiles)
    band = piece * sub_count
    tile, sub = lax.axis_index("tile"), lax.axis_index("sub")
    if depth_count > 1:
        here = keep_ref[...] + relay_ref[: 2 * count, :]
        there = core_ref[...] + chip_ref[2 * count :, :]
    else:
        here, there = keep_ref[...], core_ref[...]
    summed = jnp.concatenate([here[:count], there[:count], here[count:], there[count:]], axis=0)
    pair = (summed * (1.0 / total_seqs) + out_bias[...]).astype(jnp.bfloat16)
    values = pair.astype(jnp.float32)
    center = jnp.mean(values, axis=-1, keepdims=True)
    shifted = values - center
    spread = jnp.mean(shifted * shifted, axis=-1, keepdims=True)
    normed = (shifted * lax.rsqrt(spread + 1e-05)).astype(jnp.bfloat16)
    gate = jnp.dot(normed, gate_weight[...], preferred_element_type=jnp.float32)
    up = jnp.dot(normed, up_weight[...], preferred_element_type=jnp.float32)
    hidden = (jax.nn.silu(gate) * up).astype(jnp.bfloat16)
    moved = (values + jnp.dot(hidden, down_weight[...], preferred_element_type=jnp.float32)).astype(jnp.bfloat16)
    moved = moved.astype(jnp.float32)
    symmetric = ((moved[: 2 * count] + moved[2 * count :]) * 0.5).astype(jnp.bfloat16)
    packed = LANES // bins
    weight = jnp.concatenate([bins_weight[...]] * packed, axis=0)
    bias = jnp.concatenate([bins_bias[...]] * packed, axis=1)
    logits = lax.dot_general(symmetric, weight, NT, preferred_element_type=jnp.float32) + bias
    lane = lax.broadcasted_iota(jnp.int32, (1, LANES), 1)
    symmetric = symmetric.astype(jnp.float32)
    for side in range(2):
        for k, bits in enumerate(block_tiles):
            half = sub ^ (parity(bits) ^ side)
            start = (tile ^ bits) * band + half * piece
            row = side * count + k * piece
            for j in range(piece):
                at = pl.multiple_of((start + j) * pair_channels, pair_channels)
                symmetric_out[:, pl.ds(at, pair_channels)] = symmetric[row + j : row + j + 1].astype(jnp.bfloat16)
            for j in range(0, piece, packed):
                line = logits[row + j : row + j + 1]
                for p in range(1, packed):
                    line = jnp.where(lane < p * bins, line, logits[row + j + p : row + j + p + 1])
                at = pl.multiple_of((start + j) * bins, LANES)
                bins_out[:, pl.ds(at, LANES)] = line


def cost(flops, size):
    return pl.CostEstimate(flops=flops, bytes_accessed=size, transcendentals=0)


def shape(rows, columns, kind):
    return jax.ShapeDtypeStruct((rows, columns), kind)


def per_device(
    left_mantissa,
    left_exponent,
    right_mantissa,
    right_exponent,
    residue_mask,
    out_weight,
    out_bias,
    gate_weight,
    up_weight,
    down_weight,
    distogram_weight,
    distogram_bias,
):
    tile_count, depth_count, sub_count = (lax.axis_size(a) for a in GROUP)
    seqs, width = left_mantissa.shape
    band = left_exponent.shape[1]
    piece = right_exponent.shape[1]
    channels = width // band
    fold = channels // ROWS
    residues = residue_mask.shape[0]
    pair_channels = out_weight.shape[1]
    bins = distogram_weight.shape[1]
    if sub_count != 2 or band != depth_count * sub_count or tile_count & (tile_count - 1) or band & (band - 1):
        raise ValueError("unsupported mesh")
    dims = (channels, depth_count, sub_count)
    bf16, f32 = jnp.bfloat16, jnp.float32

    own, left_rows, right_rows = pl.pallas_call(
        functools.partial(prepare_kernel, dims),
        out_shape=(
            shape(2 * piece * channels, seqs, bf16),
            shape(band * channels, seqs, bf16),
            shape(piece * channels, seqs, bf16),
        ),
        in_specs=[VMEM] * 4 + [SMEM],
        out_specs=(VMEM,) * 3,
        scratch_shapes=[pltpu.VMEM((band * channels, seqs), f32)],
        cost_estimate=cost(1 << 16, 1 << 17),
        name="prepare",
    )(left_mantissa, left_exponent.T, right_mantissa.T, right_exponent.T, residue_mask)
    blocks = {0: own}
    for bit in bits_of(tile_count):
        for bits in list(blocks):
            blocks[bits ^ bit] = xor_permute(blocks[bits], bit, 0, 1)
    other_rows = xor_permute(right_rows, 0, 0, 1)
    left_spread, right_spread, swapped = pl.pallas_call(
        functools.partial(spread_kernel, dims),
        out_shape=(
            shape(band * fold * channels, fold * seqs, bf16),
            shape(band * fold * channels, fold * seqs, bf16),
            shape(*out_weight.shape, bf16),
        ),
        in_specs=[VMEM] * 4,
        out_specs=(VMEM,) * 3,
        scratch_shapes=[pltpu.VMEM((sub_count, piece, channels, seqs), bf16), pltpu.VMEM(out_weight.shape, f32)],
        cost_estimate=cost(1 << 16, 1 << 20),
        name="spread",
    )(left_rows, right_rows, other_rows, out_weight)
    block_tiles = tuple(sorted(blocks))
    count = len(block_tiles) * piece
    keep, core, chip = pl.pallas_call(
        functools.partial(pair_kernel, dims, len(block_tiles)),
        out_shape=(
            shape(2 * count, pair_channels, f32),
            shape(2 * count, pair_channels, f32),
            shape(max(band - sub_count, 1) * 2 * count, pair_channels, f32),
        ),
        in_specs=[VMEM] * (len(block_tiles) + 4),
        out_specs=(VMEM,) * 3,
        scratch_shapes=[pltpu.VMEM((2 * band, count * ROWS, fold * channels), f32)],
        cost_estimate=cost(1 << 27, 1 << 21),
        name="pair",
    )(*(blocks[k] for k in block_tiles), left_spread, right_spread, out_weight, swapped)
    size = sub_count * 2 * count
    for bit in bits_of(depth_count)[:-1]:
        rows = jnp.concatenate([keep, core, chip], axis=0)
        rows = rows.reshape(-1, 2, bit, size // sub_count * sub_count, pair_channels)[0]
        mine = rows[0] + xor_permute(rows[1], 0, bit, 0)
        mine = mine.reshape(-1, pair_channels)
        keep, core, chip = mine[: size // 2], mine[size // 2 : size], mine[size:]
    from_chip = xor_permute(chip, 0, 1, 1) if depth_count > 1 else chip
    from_core = xor_permute(core, 0, 0, 1)
    relayed = xor_permute(from_chip[: 2 * count], 0, 0, 1) if depth_count > 1 else from_core
    return pl.pallas_call(
        functools.partial(finish_kernel, dims, block_tiles, seqs * depth_count),
        out_shape=(shape(1, residues * pair_channels, bf16), shape(1, residues * bins, f32)),
        in_specs=[VMEM] * 10,
        out_specs=(VMEM, VMEM),
        cost_estimate=cost(1 << 25, 1 << 20),
        name="finish",
    )(
        keep,
        from_core,
        from_chip,
        relayed,
        out_bias.reshape(1, -1),
        gate_weight,
        up_weight,
        down_weight,
        distogram_weight.T,
        distogram_bias.reshape(1, -1),
    )


def solution(mesh):
    in_specs = (
        P(("parts", "depth"), "tile"),
        P(("parts", "depth"), "tile"),
        P(("parts", "depth"), ("tile", "sub")),
        P(("parts", "depth"), ("tile", "sub")),
        P("parts"),
        P(),
        P(),
        P(),
        P(),
        P(),
        P(),
        P(),
    )
    out_specs = (
        P(("parts", "tile", "depth", "sub"), None),
        P(("parts", "tile", "depth", "sub"), None),
    )
    step = jax.shard_map(
        per_device, mesh=mesh, in_specs=in_specs, out_specs=out_specs, check_vma=False
    )
    known = [0]
    for bit in bits_of(mesh.shape["tile"]):
        for bits in list(known):
            known.append(bits ^ bit)
    return step
```

```python
import functools
import math

import jax
import jax.numpy as jnp
from jax import lax
from jax.experimental import pallas as pl
from jax.experimental.pallas import tpu as pltpu
from jax.sharding import PartitionSpec as P


LANES = 128
ROWS = 8
GROUP = ("tile", "depth", "sub")
NT = (((1,), (1,)), ((), ()))
VMEM = pl.BlockSpec(memory_space=pltpu.VMEM)
HBM = pl.BlockSpec(memory_space=pltpu.HBM)


def parity(number):
    return bin(number).count("1") & 1


def xor_permute(value, tile_bits, depth_bits, sub_bits):
    depth_count, sub_count = lax.axis_size("depth"), lax.axis_size("sub")
    pairs = []
    for t in range(lax.axis_size("tile")):
        for d in range(depth_count):
            for s in range(sub_count):
                here = (t * depth_count + d) * sub_count + s
                there = ((t ^ tile_bits) * depth_count + (d ^ depth_bits)) * sub_count + (s ^ sub_bits)
                pairs.append((here, there))
    return lax.ppermute(value, GROUP, pairs)


def bits_of(count):
    return [1 << b for b in reversed(range(count.bit_length() - 1))]


def row_in_tile(sub_count):
    return lax.axis_index("depth") * sub_count + lax.axis_index("sub")


def prepare_kernel(dims, *refs):
    channels, _, sub_count = dims
    params = (len(refs) - 15) // 2
    sources, refs = refs[: 5 + params], refs[5 + params :]
    block_ref, left_out, right_out = refs[:3]
    params_out, refs = refs[3 : 3 + params], refs[3 + params :]
    left_ref, left_exp_ref, right_ref, right_exp_ref, mask_ref, left_f32, semaphores = refs
    copies = [
        pltpu.make_async_copy(source, target, semaphores.at[n])
        for n, (source, target) in enumerate(
            zip(sources, (left_ref, left_exp_ref, right_ref, right_exp_ref, mask_ref, *params_out))
        )
    ]
    for copy in copies:
        copy.start()
    for copy in copies[:5]:
        copy.wait()
    band = left_exp_ref.shape[0]
    piece = right_exp_ref.shape[0]
    fold = channels // ROWS
    tile, sub = lax.axis_index("tile"), lax.axis_index("sub")
    mine = row_in_tile(sub_count)
    right = right_ref[...].astype(jnp.float32)
    right_scale = jnp.exp2(right_exp_ref[...].astype(jnp.float32))
    first = tile * band + sub * piece
    scaled = []
    for j in range(piece):
        scale = right_scale[j : j + 1] * mask_ref[first + j].astype(jnp.float32)
        scaled.append(right[j * channels : (j + 1) * channels] * scale)
        right_out[j * channels : (j + 1) * channels, :] = scaled[j].astype(jnp.bfloat16)
    half = fold * piece * ROWS
    for x in range(fold):
        rows = jnp.concatenate([scaled[j][x * ROWS : (x + 1) * ROWS] for j in range(piece)], axis=0)
        at = half + x * piece * ROWS
        block_ref[at : at + piece * ROWS, :] = rows.astype(jnp.bfloat16)
    left = jnp.transpose(left_ref[...].astype(jnp.float32))
    left_scale = jnp.exp2(left_exp_ref[...].astype(jnp.float32))
    for i in range(band):
        scale = left_scale[i : i + 1] * mask_ref[tile * band + i].astype(jnp.float32)
        left_f32[i * channels : (i + 1) * channels, :] = left[i * channels : (i + 1) * channels] * scale
    for x in range(fold):
        rows = []
        for j in range(piece):
            at = pl.multiple_of((sub * piece + j) * channels + x * ROWS, ROWS)
            rows.append(left_f32[pl.ds(at, ROWS), :])
        at = x * piece * ROWS
        block_ref[at : at + piece * ROWS, :] = jnp.concatenate(rows, axis=0).astype(jnp.bfloat16)
    for i in range(band):
        at = pl.multiple_of((mine ^ i) * channels, channels)
        left_out[i * channels : (i + 1) * channels, :] = left_f32[pl.ds(at, channels), :].astype(jnp.bfloat16)
    for copy in copies[5:]:
        copy.wait()


def spread_kernel(
    dims, left_ref, right_ref, other_ref, weight_ref, left_spread, right_spread, weight_out, both, weight_f32
):
    channels, _, sub_count = dims
    seqs = left_ref.shape[1]
    band = left_ref.shape[0] // channels
    piece = right_ref.shape[0] // channels
    fold = channels // ROWS
    sub = lax.axis_index("sub")
    mine = row_in_tile(sub_count)
    both[sub] = right_ref[...].reshape(piece, channels, seqs)
    both[1 - sub] = other_ref[...].reshape(piece, channels, seqs)
    left_spread[...] = jnp.zeros_like(left_spread)
    right_spread[...] = jnp.zeros_like(right_spread)
    for i in range(band):
        here = mine ^ i
        left = left_ref[i * channels : (i + 1) * channels, :]
        right = both[here // piece, here % piece]
        for x in range(fold):
            at = (i * fold + x) * channels
            left_spread[at : at + channels, x * seqs : (x + 1) * seqs] = left
            right_spread[at : at + channels, x * seqs : (x + 1) * seqs] = right
    weight_f32[...] = weight_ref[...].astype(jnp.float32)
    for g in range(ROWS):
        for x in range(fold):
            at = (g * fold + x) * channels
            rows = weight_f32[pl.ds(x * ROWS + g, channels, stride=channels), :]
            weight_out[at : at + channels, :] = rows.astype(jnp.bfloat16)


def pair_kernel(dims, block_count, *refs):
    channels, _, sub_count = dims
    blocks = refs[:block_count]
    left_spread, right_spread, weight_ref, swapped_ref, keep_ref, core_ref, chip_ref, outer = refs[block_count:]
    fold = channels // ROWS
    half = blocks[0].shape[0] // 2
    size = half // fold
    piece = size // ROWS
    count = block_count * piece
    band = left_spread.shape[0] // (fold * channels)
    width = fold * channels
    natural = jnp.concatenate(
        [
            weight_ref[(x * ROWS + g) * channels : (x * ROWS + g + 1) * channels, :]
            for g in range(ROWS)
            for x in range(fold)
        ],
        axis=0,
    )
    for way in range(2):
        base = half * (1 - way)
        factor = jnp.concatenate(
            [
                jnp.concatenate([b[base + x * size : base + (x + 1) * size, :] for b in blocks], axis=0)
                for x in range(fold)
            ],
            axis=1,
        )
        spread = left_spread if way == 0 else right_spread
        product = lax.dot_general(factor, spread[...], NT, preferred_element_type=jnp.float32)
        for i in range(band):
            outer[way * band + i] = product[:, i * width : (i + 1) * width]
        flat = jnp.concatenate(
            [
                jnp.concatenate(
                    [outer[way * band + i, pl.ds(g, count, stride=ROWS), :] for g in range(ROWS)],
                    axis=1,
                )
                for i in range(band)
            ],
            axis=0,
        )
        high = flat.astype(jnp.bfloat16)
        low = (flat - high.astype(jnp.float32)).astype(jnp.bfloat16)
        weight = swapped_ref[...] if way == 0 else natural
        terms = jnp.dot(jnp.concatenate([high, low], axis=0), weight, preferred_element_type=jnp.float32)
        terms = terms[: band * count] + terms[band * count :]
        place = lambda i: slice(i * count, (i + 1) * count)
        keep_ref[place(way), :] = terms[place(0)]
        core_ref[place(way), :] = terms[place(1)]
        for i in range(sub_count, band):
            chip_ref[place((i - sub_count) * 2 + way), :] = terms[place(i)]


def finish_kernel(
    dims,
    block_tiles,
    total_seqs,
    keep_ref,
    core_ref,
    chip_ref,
    relay_ref,
    out_bias,
    gate_weight,
    up_weight,
    down_weight,
    bins_weight,
    bins_bias,
    symmetric_out,
    bins_out,
):
    _, depth_count, sub_count = dims
    pair_channels = gate_weight.shape[0]
    bins = bins_weight.shape[0]
    count = keep_ref.shape[0] // 2
    piece = count // len(block_tiles)
    band = piece * sub_count
    tile, sub = lax.axis_index("tile"), lax.axis_index("sub")
    if depth_count > 1:
        here = keep_ref[...] + relay_ref[: 2 * count, :]
        there = core_ref[...] + chip_ref[2 * count :, :]
    else:
        here, there = keep_ref[...], core_ref[...]
    summed = jnp.concatenate([here[:count], there[:count], here[count:], there[count:]], axis=0)
    pair = (summed * (1.0 / total_seqs) + out_bias[...]).astype(jnp.bfloat16)
    values = pair.astype(jnp.float32)
    center = jnp.mean(values, axis=-1, keepdims=True)
    shifted = values - center
    spread = jnp.mean(shifted * shifted, axis=-1, keepdims=True)
    normed = (shifted * lax.rsqrt(spread + 1e-05)).astype(jnp.bfloat16)
    gate = jnp.dot(normed, gate_weight[...], preferred_element_type=jnp.float32)
    up = jnp.dot(normed, up_weight[...], preferred_element_type=jnp.float32)
    hidden = (jax.nn.silu(gate) * up).astype(jnp.bfloat16)
    moved = (values + jnp.dot(hidden, down_weight[...], preferred_element_type=jnp.float32)).astype(jnp.bfloat16)
    moved = moved.astype(jnp.float32)
    symmetric = ((moved[: 2 * count] + moved[2 * count :]) * 0.5).astype(jnp.bfloat16)
    packed = LANES // bins
    weight = jnp.concatenate([bins_weight[...]] * packed, axis=0)
    bias = jnp.concatenate([bins_bias[...]] * packed, axis=1)
    logits = lax.dot_general(symmetric, weight, NT, preferred_element_type=jnp.float32) + bias
    lane = lax.broadcasted_iota(jnp.int32, (1, LANES), 1)
    symmetric = symmetric.astype(jnp.float32)
    for side in range(2):
        for k, bits in enumerate(block_tiles):
            half = sub ^ (parity(bits) ^ side)
            start = (tile ^ bits) * band + half * piece
            row = side * count + k * piece
            for j in range(piece):
                at = pl.multiple_of((start + j) * pair_channels, pair_channels)
                symmetric_out[:, pl.ds(at, pair_channels)] = symmetric[row + j : row + j + 1].astype(jnp.bfloat16)
            for j in range(0, piece, packed):
                line = logits[row + j : row + j + 1]
                for p in range(1, packed):
                    line = jnp.where(lane < p * bins, line, logits[row + j + p : row + j + p + 1])
                at = pl.multiple_of((start + j) * bins, LANES)
                bins_out[:, pl.ds(at, LANES)] = line


def call(kernel, flops, outs, scratch, operands, place=VMEM):
    arrays = [(a.shape, a.dtype) for a in (*operands, *outs)]
    arrays += [(a.shape, a.dtype) for a in scratch if a.memory_space == pltpu.VMEM]
    size = sum(math.prod(dims) * jnp.dtype(kind).itemsize for dims, kind in arrays)
    return pl.pallas_call(
        kernel,
        out_shape=outs,
        in_specs=[place] * len(operands),
        out_specs=(VMEM,) * len(outs),
        scratch_shapes=scratch,
        compiler_params=pltpu.CompilerParams(vmem_limit_bytes=min(2 * size + (2 << 20), 60 << 20)),
        cost_estimate=pl.CostEstimate(flops=flops, bytes_accessed=size, transcendentals=0),
    )(*(pltpu.with_memory_space_constraint(a, pltpu.HBM) if place is HBM else a for a in operands))


def shape(rows, columns, kind):
    return jax.ShapeDtypeStruct((rows, columns), kind)


def per_device(
    left_mantissa,
    left_exponent,
    right_mantissa,
    right_exponent,
    residue_mask,
    out_weight,
    out_bias,
    gate_weight,
    up_weight,
    down_weight,
    distogram_weight,
    distogram_bias,
):
    tile_count, depth_count, sub_count = (lax.axis_size(a) for a in GROUP)
    seqs, width = left_mantissa.shape
    band = left_exponent.shape[1]
    piece = right_exponent.shape[1]
    channels = width // band
    fold = channels // ROWS
    residues = residue_mask.shape[0]
    pair_channels = out_weight.shape[1]
    bins = distogram_weight.shape[1]
    if sub_count != 2 or band != depth_count * sub_count or tile_count & (tile_count - 1) or band & (band - 1):
        raise ValueError("unsupported mesh")
    dims = (channels, depth_count, sub_count)
    bf16, f32 = jnp.bfloat16, jnp.float32

    sources = (left_mantissa, left_exponent.T, right_mantissa.T, right_exponent.T, residue_mask)
    params = (
        out_weight,
        out_bias.reshape(1, -1),
        gate_weight,
        up_weight,
        down_weight,
        distogram_weight.T,
        distogram_bias.reshape(1, -1),
    )
    own, left_rows, right_rows, *params = call(
        functools.partial(prepare_kernel, dims),
        1 << 16,
        (
            shape(2 * piece * channels, seqs, bf16),
            shape(band * channels, seqs, bf16),
            shape(piece * channels, seqs, bf16),
            *(shape(*p.shape, p.dtype) for p in params),
        ),
        [pltpu.VMEM(s.shape, s.dtype) for s in sources[:4]]
        + [
            pltpu.SMEM(residue_mask.shape, residue_mask.dtype),
            pltpu.VMEM((band * channels, seqs), f32),
            pltpu.SemaphoreType.DMA((len(sources) + len(params),)),
        ],
        (*sources, *params),
        HBM,
    )
    out_weight = params[0]
    blocks = {0: own}
    for bit in bits_of(tile_count):
        for bits in list(blocks):
            blocks[bits ^ bit] = xor_permute(blocks[bits], bit, 0, 1)
    other_rows = xor_permute(right_rows, 0, 0, 1)
    left_spread, right_spread, swapped = call(
        functools.partial(spread_kernel, dims),
        1 << 16,
        (
            shape(band * fold * channels, fold * seqs, bf16),
            shape(band * fold * channels, fold * seqs, bf16),
            shape(*out_weight.shape, bf16),
        ),
        [pltpu.VMEM((sub_count, piece, channels, seqs), bf16), pltpu.VMEM(out_weight.shape, f32)],
        (left_rows, right_rows, other_rows, out_weight),
    )
    block_tiles = tuple(sorted(blocks))
    count = len(block_tiles) * piece
    keep, core, chip = call(
        functools.partial(pair_kernel, dims, len(block_tiles)),
        1 << 27,
        (
            shape(2 * count, pair_channels, f32),
            shape(2 * count, pair_channels, f32),
            shape(max(band - sub_count, 1) * 2 * count, pair_channels, f32),
        ),
        [pltpu.VMEM((2 * band, count * ROWS, fold * channels), f32)],
        (*(blocks[k] for k in block_tiles), left_spread, right_spread, out_weight, swapped),
    )
    size = sub_count * 2 * count
    for bit in bits_of(depth_count)[:-1]:
        rows = jnp.concatenate([keep, core, chip], axis=0)
        rows = rows.reshape(-1, 2, bit, size // sub_count * sub_count, pair_channels)[0]
        mine = rows[0] + xor_permute(rows[1], 0, bit, 0)
        mine = mine.reshape(-1, pair_channels)
        keep, core, chip = mine[: size // 2], mine[size // 2 : size], mine[size:]
    from_chip = xor_permute(chip, 0, 1, 1) if depth_count > 1 else chip
    from_core = xor_permute(core, 0, 0, 1)
    relayed = xor_permute(from_chip[: 2 * count], 0, 0, 1) if depth_count > 1 else from_core
    return call(
        functools.partial(finish_kernel, dims, block_tiles, seqs * depth_count),
        1 << 25,
        (shape(1, residues * pair_channels, bf16), shape(1, residues * bins, f32)),
        [],
        (
            keep,
            from_core,
            from_chip,
            relayed,
            *params[1:],
        ),
    )


def solution(mesh):
    in_specs = (
        P(("parts", "depth"), "tile"),
        P(("parts", "depth"), "tile"),
        P(("parts", "depth"), ("tile", "sub")),
        P(("parts", "depth"), ("tile", "sub")),
        P("parts"),
        P(),
        P(),
        P(),
        P(),
        P(),
        P(),
        P(),
    )
    out_specs = (
        P(("parts", "tile", "depth", "sub"), None),
        P(("parts", "tile", "depth", "sub"), None),
    )
    step = jax.shard_map(
        per_device, mesh=mesh, in_specs=in_specs, out_specs=out_specs, check_vma=False
    )
    known = [0]
    for bit in bits_of(mesh.shape["tile"]):
        for bits in list(known):
            known.append(bits ^ bit)
    return step
```

```python
import functools
import math

import jax
import jax.numpy as jnp
from jax import lax
from jax.experimental import pallas as pl
from jax.experimental.pallas import tpu as pltpu
from jax.sharding import PartitionSpec as P


LANES = 128
ROWS = 8
GROUP = ("tile", "depth", "sub")
NT = (((1,), (1,)), ((), ()))
VMEM = pl.BlockSpec(memory_space=pltpu.VMEM)
HBM = pl.BlockSpec(memory_space=pltpu.HBM)


def parity(number):
    return bin(number).count("1") & 1


def xor_permute(value, tile_bits, depth_bits, sub_bits):
    depth_count, sub_count = lax.axis_size("depth"), lax.axis_size("sub")
    pairs = []
    for t in range(lax.axis_size("tile")):
        for d in range(depth_count):
            for s in range(sub_count):
                here = (t * depth_count + d) * sub_count + s
                there = ((t ^ tile_bits) * depth_count + (d ^ depth_bits)) * sub_count + (s ^ sub_bits)
                pairs.append((here, there))
    return lax.ppermute(value, GROUP, pairs)


def bits_of(count):
    return [1 << b for b in reversed(range(count.bit_length() - 1))]


def row_in_tile(sub_count):
    return lax.axis_index("depth") * sub_count + lax.axis_index("sub")


def fetch(sources, targets, semaphores):
    copies = [
        pltpu.make_async_copy(source, target, semaphores.at[n])
        for n, (source, target) in enumerate(zip(sources, targets))
    ]
    for copy in copies:
        copy.start()
    return copies


def prepare_kernel(dims, *refs):
    channels, _, sub_count = dims
    sources, (block_ref, left_out, right_out), scratch = refs[:5], refs[5:8], refs[8:]
    left_ref, left_exp_ref, right_ref, right_exp_ref, mask_ref, left_f32, semaphores = scratch
    for copy in fetch(sources, scratch, semaphores):
        copy.wait()
    band = left_exp_ref.shape[0]
    piece = right_exp_ref.shape[0]
    fold = channels // ROWS
    tile, sub = lax.axis_index("tile"), lax.axis_index("sub")
    mine = row_in_tile(sub_count)
    right = right_ref[...].astype(jnp.float32)
    right_scale = jnp.exp2(right_exp_ref[...].astype(jnp.float32))
    first = tile * band + sub * piece
    scaled = []
    for j in range(piece):
        scale = right_scale[j : j + 1] * mask_ref[first + j].astype(jnp.float32)
        scaled.append(right[j * channels : (j + 1) * channels] * scale)
        right_out[j * channels : (j + 1) * channels, :] = scaled[j].astype(jnp.bfloat16)
    half = fold * piece * ROWS
    for x in range(fold):
        rows = jnp.concatenate([scaled[j][x * ROWS : (x + 1) * ROWS] for j in range(piece)], axis=0)
        at = half + x * piece * ROWS
        block_ref[at : at + piece * ROWS, :] = rows.astype(jnp.bfloat16)
    left = jnp.transpose(left_ref[...].astype(jnp.float32))
    left_scale = jnp.exp2(left_exp_ref[...].astype(jnp.float32))
    for i in range(band):
        scale = left_scale[i : i + 1] * mask_ref[tile * band + i].astype(jnp.float32)
        left_f32[i * channels : (i + 1) * channels, :] = left[i * channels : (i + 1) * channels] * scale
    for x in range(fold):
        rows = []
        for j in range(piece):
            at = pl.multiple_of((sub * piece + j) * channels + x * ROWS, ROWS)
            rows.append(left_f32[pl.ds(at, ROWS), :])
        at = x * piece * ROWS
        block_ref[at : at + piece * ROWS, :] = jnp.concatenate(rows, axis=0).astype(jnp.bfloat16)
    for i in range(band):
        at = pl.multiple_of((mine ^ i) * channels, channels)
        left_out[i * channels : (i + 1) * channels, :] = left_f32[pl.ds(at, channels), :].astype(jnp.bfloat16)


def arrange_kernel(dims, *refs):
    channels, _, sub_count = dims
    params = (len(refs) - 7) // 2
    right_ref, other_ref = refs[:2]
    sources, refs = refs[2 : 2 + params], refs[2 + params :]
    right_out, swapped_out = refs[:2]
    targets, (both, weight_f32, semaphores) = refs[2 : 2 + params], refs[2 + params :]
    copies = fetch(sources, targets, semaphores)
    seqs = right_ref.shape[1]
    piece = right_ref.shape[0] // channels
    fold = channels // ROWS
    sub = lax.axis_index("sub")
    mine = row_in_tile(sub_count)
    both[sub] = right_ref[...].reshape(piece, channels, seqs)
    both[1 - sub] = other_ref[...].reshape(piece, channels, seqs)
    for i in range(right_out.shape[0] // channels):
        here = mine ^ i
        right_out[i * channels : (i + 1) * channels, :] = both[here // piece, here % piece]
    copies[0].wait()
    weight_f32[...] = targets[0][...].astype(jnp.float32)
    for g in range(ROWS):
        for x in range(fold):
            at = (g * fold + x) * channels
            rows = weight_f32[pl.ds(x * ROWS + g, channels, stride=channels), :]
            swapped_out[at : at + channels, :] = rows.astype(jnp.bfloat16)
    for copy in copies[1:]:
        copy.wait()


def trade_chunks(arrays, width):
    chunk = lax.broadcasted_iota(jnp.int32, arrays[0].shape, 1) // width
    for bit in bits_of(len(arrays)):
        keep = (chunk & bit) == 0
        for x in range(len(arrays)):
            if x & bit:
                continue
            low, high = arrays[x], arrays[x | bit]
            arrays[x] = jnp.where(keep, low, pltpu.roll(high, bit * width, 1))
            arrays[x | bit] = jnp.where(keep, pltpu.roll(low, LANES - bit * width, 1), high)
    return arrays


def pair_kernel(dims, block_count, *refs):
    channels, _, sub_count = dims
    blocks = refs[:block_count]
    left_ref, right_ref, weight_ref, swapped_ref, keep_ref, core_ref, chip_ref, outer = refs[block_count:]
    fold = channels // ROWS
    half = blocks[0].shape[0] // 2
    size = half // fold
    count = block_count * size // ROWS
    rows = count * ROWS
    band = left_ref.shape[0] // channels
    for way, own in enumerate((left_ref, right_ref)):
        base = half * (1 - way)
        factor = jnp.concatenate(
            [b[base + x * size : base + (x + 1) * size, :] for x in range(fold) for b in blocks], axis=0
        )
        product = lax.dot_general(factor, own[...], NT, preferred_element_type=jnp.float32)
        for i in range(0, band, fold):
            lanes = slice(i * channels, i * channels + LANES)
            parts = [product[x * rows : (x + 1) * rows, lanes] for x in range(fold)]
            for n, part in enumerate(trade_chunks(parts, channels)):
                outer[way * band + i + n] = part
    natural = jnp.concatenate(
        [
            weight_ref[(x * ROWS + g) * channels : (x * ROWS + g + 1) * channels, :]
            for g in range(ROWS)
            for x in range(fold)
        ],
        axis=0,
    )
    for way, weight in enumerate((swapped_ref[...], natural)):
        flat = jnp.concatenate(
            [
                jnp.concatenate(
                    [outer[way * band + i, pl.ds(g, count, stride=ROWS), :] for g in range(ROWS)],
                    axis=1,
                )
                for i in range(band)
            ],
            axis=0,
        )
        high = flat.astype(jnp.bfloat16)
        low = (flat - high.astype(jnp.float32)).astype(jnp.bfloat16)
        terms = jnp.dot(jnp.concatenate([high, low], axis=0), weight, preferred_element_type=jnp.float32)
        terms = terms[: band * count] + terms[band * count :]
        place = lambda i: slice(i * count, (i + 1) * count)
        keep_ref[place(way), :] = terms[place(0)]
        core_ref[place(way), :] = terms[place(1)]
        for i in range(sub_count, band):
            chip_ref[place((i - sub_count) * 2 + way), :] = terms[place(i)]


def finish_kernel(
    dims,
    block_tiles,
    total_seqs,
    keep_ref,
    core_ref,
    chip_ref,
    relay_ref,
    out_bias,
    gate_weight,
    up_weight,
    down_weight,
    bins_weight,
    bins_bias,
    symmetric_out,
    bins_out,
):
    _, depth_count, sub_count = dims
    pair_channels = gate_weight.shape[0]
    bins = bins_weight.shape[0]
    count = keep_ref.shape[0] // 2
    piece = count // len(block_tiles)
    band = piece * sub_count
    tile, sub = lax.axis_index("tile"), lax.axis_index("sub")
    if depth_count > 1:
        here = keep_ref[...] + relay_ref[: 2 * count, :]
        there = core_ref[...] + chip_ref[2 * count :, :]
    else:
        here, there = keep_ref[...], core_ref[...]
    summed = jnp.concatenate([here[:count], there[:count], here[count:], there[count:]], axis=0)
    pair = (summed * (1.0 / total_seqs) + out_bias[...]).astype(jnp.bfloat16)
    values = pair.astype(jnp.float32)
    center = jnp.mean(values, axis=-1, keepdims=True)
    shifted = values - center
    spread = jnp.mean(shifted * shifted, axis=-1, keepdims=True)
    normed = (shifted * lax.rsqrt(spread + 1e-05)).astype(jnp.bfloat16)
    gate = jnp.dot(normed, gate_weight[...], preferred_element_type=jnp.float32)
    up = jnp.dot(normed, up_weight[...], preferred_element_type=jnp.float32)
    hidden = (jax.nn.silu(gate) * up).astype(jnp.bfloat16)
    moved = (values + jnp.dot(hidden, down_weight[...], preferred_element_type=jnp.float32)).astype(jnp.bfloat16)
    moved = moved.astype(jnp.float32)
    symmetric = ((moved[: 2 * count] + moved[2 * count :]) * 0.5).astype(jnp.bfloat16)
    packed = LANES // bins
    weight = jnp.concatenate([bins_weight[...]] * packed, axis=0)
    bias = jnp.concatenate([bins_bias[...]] * packed, axis=1)
    logits = lax.dot_general(symmetric, weight, NT, preferred_element_type=jnp.float32) + bias
    lane = lax.broadcasted_iota(jnp.int32, (1, LANES), 1)
    symmetric = symmetric.astype(jnp.float32)
    for side in range(2):
        for k, bits in enumerate(block_tiles):
            half = sub ^ (parity(bits) ^ side)
            start = (tile ^ bits) * band + half * piece
            row = side * count + k * piece
            for j in range(piece):
                at = pl.multiple_of((start + j) * pair_channels, pair_channels)
                symmetric_out[:, pl.ds(at, pair_channels)] = symmetric[row + j : row + j + 1].astype(jnp.bfloat16)
            for j in range(0, piece, packed):
                line = logits[row + j : row + j + 1]
                for p in range(1, packed):
                    line = jnp.where(lane < p * bins, line, logits[row + j + p : row + j + p + 1])
                at = pl.multiple_of((start + j) * bins, LANES)
                bins_out[:, pl.ds(at, LANES)] = line


def call(kernel, flops, outs, scratch, operands, sources=()):
    arrays = [(a.shape, a.dtype) for a in (*operands, *outs)]
    arrays += [(a.shape, a.dtype) for a in scratch if a.memory_space == pltpu.VMEM]
    size = sum(math.prod(dims) * jnp.dtype(kind).itemsize for dims, kind in arrays)
    return pl.pallas_call(
        kernel,
        out_shape=outs,
        in_specs=[VMEM] * len(operands) + [HBM] * len(sources),
        out_specs=(VMEM,) * len(outs),
        scratch_shapes=scratch,
        compiler_params=pltpu.CompilerParams(vmem_limit_bytes=min(2 * size + (2 << 20), 60 << 20)),
        cost_estimate=pl.CostEstimate(flops=flops, bytes_accessed=size, transcendentals=0),
    )(*operands, *(pltpu.with_memory_space_constraint(s, pltpu.HBM) for s in sources))


def shape(rows, columns, kind):
    return jax.ShapeDtypeStruct((rows, columns), kind)


def per_device(
    left_mantissa,
    left_exponent,
    right_mantissa,
    right_exponent,
    residue_mask,
    out_weight,
    out_bias,
    gate_weight,
    up_weight,
    down_weight,
    distogram_weight,
    distogram_bias,
):
    tile_count, depth_count, sub_count = (lax.axis_size(a) for a in GROUP)
    seqs, width = left_mantissa.shape
    band = left_exponent.shape[1]
    piece = right_exponent.shape[1]
    channels = width // band
    fold = channels // ROWS
    residues = residue_mask.shape[0]
    pair_channels = out_weight.shape[1]
    bins = distogram_weight.shape[1]
    if channels * fold != LANES or band % fold or sub_count != 2 or band != depth_count * sub_count or tile_count & (tile_count - 1) or band & (band - 1):
        raise ValueError("unsupported mesh")
    dims = (channels, depth_count, sub_count)
    bf16, f32 = jnp.bfloat16, jnp.float32

    sources = (left_mantissa, left_exponent.T, right_mantissa.T, right_exponent.T, residue_mask)
    own, left_rows, right_rows = call(
        functools.partial(prepare_kernel, dims),
        1 << 16,
        (
            shape(2 * piece * channels, seqs, bf16),
            shape(band * channels, seqs, bf16),
            shape(piece * channels, seqs, bf16),
        ),
        [pltpu.VMEM(s.shape, s.dtype) for s in sources[:4]]
        + [
            pltpu.SMEM(residue_mask.shape, residue_mask.dtype),
            pltpu.VMEM((band * channels, seqs), f32),
            pltpu.SemaphoreType.DMA((len(sources),)),
        ],
        (),
        sources,
    )
    blocks = {0: own}
    for bit in bits_of(tile_count):
        for bits in list(blocks):
            blocks[bits ^ bit] = xor_permute(blocks[bits], bit, 0, 1)
    other_rows = xor_permute(right_rows, 0, 0, 1)
    params = (
        out_weight,
        out_bias.reshape(1, -1),
        gate_weight,
        up_weight,
        down_weight,
        distogram_weight.T,
        distogram_bias.reshape(1, -1),
    )
    right_rows, swapped, weight, *params = call(
        functools.partial(arrange_kernel, dims),
        1 << 16,
        (
            shape(band * channels, seqs, bf16),
            shape(*out_weight.shape, bf16),
            *(shape(*p.shape, p.dtype) for p in params),
        ),
        [
            pltpu.VMEM((sub_count, piece, channels, seqs), bf16),
            pltpu.VMEM(out_weight.shape, f32),
            pltpu.SemaphoreType.DMA((len(params),)),
        ],
        (right_rows, other_rows),
        params,
    )
    block_tiles = tuple(sorted(blocks))
    count = len(block_tiles) * piece
    keep, core, chip = call(
        functools.partial(pair_kernel, dims, len(block_tiles)),
        1 << 27,
        (
            shape(2 * count, pair_channels, f32),
            shape(2 * count, pair_channels, f32),
            shape(max(band - sub_count, 1) * 2 * count, pair_channels, f32),
        ),
        [pltpu.VMEM((2 * band, count * ROWS, LANES), f32)],
        (*(blocks[k] for k in block_tiles), left_rows, right_rows, weight, swapped),
    )
    size = sub_count * 2 * count
    for bit in bits_of(depth_count)[:-1]:
        rows = jnp.concatenate([keep, core, chip], axis=0)
        rows = rows.reshape(-1, 2, bit, size // sub_count * sub_count, pair_channels)[0]
        mine = rows[0] + xor_permute(rows[1], 0, bit, 0)
        mine = mine.reshape(-1, pair_channels)
        keep, core, chip = mine[: size // 2], mine[size // 2 : size], mine[size:]
    from_chip = xor_permute(chip, 0, 1, 1) if depth_count > 1 else chip
    from_core = xor_permute(core, 0, 0, 1)
    relayed = xor_permute(from_chip[: 2 * count], 0, 0, 1) if depth_count > 1 else from_core
    return call(
        functools.partial(finish_kernel, dims, block_tiles, seqs * depth_count),
        1 << 25,
        (shape(1, residues * pair_channels, bf16), shape(1, residues * bins, f32)),
        [],
        (
            keep,
            from_core,
            from_chip,
            relayed,
            *params,
        ),
    )


def solution(mesh):
    in_specs = (
        P(("parts", "depth"), "tile"),
        P(("parts", "depth"), "tile"),
        P(("parts", "depth"), ("tile", "sub")),
        P(("parts", "depth"), ("tile", "sub")),
        P("parts"),
        P(),
        P(),
        P(),
        P(),
        P(),
        P(),
        P(),
    )
    out_specs = (
        P(("parts", "tile", "depth", "sub"), None),
        P(("parts", "tile", "depth", "sub"), None),
    )
    step = jax.shard_map(
        per_device, mesh=mesh, in_specs=in_specs, out_specs=out_specs, check_vma=False
    )
    known = [0]
    for bit in bits_of(mesh.shape["tile"]):
        for bits in list(known):
            known.append(bits ^ bit)
    return step
```

```python
import functools
import math

import jax
import jax.numpy as jnp
from jax import lax
from jax.experimental import pallas as pl
from jax.experimental.pallas import tpu as pltpu
from jax.sharding import PartitionSpec as P


LANES = 128
ROWS = 8
GROUP = ("tile", "depth", "sub")
NT = (((1,), (1,)), ((), ()))
VMEM = pl.BlockSpec(memory_space=pltpu.VMEM)
HBM = pl.BlockSpec(memory_space=pltpu.HBM)


def parity(number):
    return bin(number).count("1") & 1


def xor_permute(value, tile_bits, depth_bits, sub_bits):
    depth_count, sub_count = lax.axis_size("depth"), lax.axis_size("sub")
    pairs = []
    for t in range(lax.axis_size("tile")):
        for d in range(depth_count):
            for s in range(sub_count):
                here = (t * depth_count + d) * sub_count + s
                there = ((t ^ tile_bits) * depth_count + (d ^ depth_bits)) * sub_count + (s ^ sub_bits)
                pairs.append((here, there))
    return lax.ppermute(value, GROUP, pairs)


def bits_of(count):
    return [1 << b for b in reversed(range(count.bit_length() - 1))]


def row_in_tile(sub_count):
    return lax.axis_index("depth") * sub_count + lax.axis_index("sub")


def fetch(sources, targets, semaphores):
    copies = [
        pltpu.make_async_copy(source, target, semaphores.at[n])
        for n, (source, target) in enumerate(zip(sources, targets))
    ]
    for copy in copies:
        copy.start()
    return copies


def prepare_kernel(dims, *refs):
    channels, _, sub_count = dims
    sources, (block_ref, left_out, right_out), scratch = refs[:5], refs[5:8], refs[8:]
    left_ref, left_exp_ref, right_ref, right_exp_ref, mask_ref, left_f32, semaphores = scratch
    for copy in fetch(sources, scratch, semaphores):
        copy.wait()
    band = left_exp_ref.shape[0]
    piece = right_exp_ref.shape[0]
    fold = channels // ROWS
    tile, sub = lax.axis_index("tile"), lax.axis_index("sub")
    mine = row_in_tile(sub_count)
    half = fold * piece * ROWS
    right = right_ref[...].astype(jnp.float32)
    right_scale = jnp.exp2(right_exp_ref[...].astype(jnp.float32))
    first = tile * band + sub * piece
    for j in range(piece):
        scale = right_scale[j : j + 1] * mask_ref[first + j].astype(jnp.float32)
        scaled = (right[j * channels : (j + 1) * channels] * scale).astype(jnp.bfloat16)
        right_out[j * channels : (j + 1) * channels, :] = scaled
        block_ref[half + j * channels : half + (j + 1) * channels, :] = scaled
    left = jnp.transpose(left_ref[...].astype(jnp.float32))
    left_scale = jnp.exp2(left_exp_ref[...].astype(jnp.float32))
    for i in range(band):
        scale = left_scale[i : i + 1] * mask_ref[tile * band + i].astype(jnp.float32)
        left_f32[i * channels : (i + 1) * channels, :] = left[i * channels : (i + 1) * channels] * scale
    for target, places in (
        (block_ref, [sub * piece + j for j in range(piece)]),
        (left_out, [mine ^ i for i in range(band)]),
    ):
        for x in range(fold):
            rows = [
                left_f32[pl.ds(pl.multiple_of(place * channels + x * ROWS, ROWS), ROWS), :] for place in places
            ]
            at = x * len(places) * ROWS
            target[at : at + len(places) * ROWS, :] = jnp.concatenate(rows, axis=0).astype(jnp.bfloat16)


def trade_chunks(arrays, width):
    chunk = lax.broadcasted_iota(jnp.int32, arrays[0].shape, 1) // width
    for bit in bits_of(len(arrays)):
        keep = (chunk & bit) == 0
        for x in range(len(arrays)):
            if x & bit:
                continue
            low, high = arrays[x], arrays[x | bit]
            arrays[x] = jnp.where(keep, low, pltpu.roll(high, bit * width, 1))
            arrays[x | bit] = jnp.where(keep, pltpu.roll(low, LANES - bit * width, 1), high)
    return arrays


def pair_terms(channels, blocks, left_ref, right_ref, weight_ref, scratch, store, ready):
    fold = channels // ROWS
    piece = (blocks[0].shape[0] // channels) // 2
    half = piece * channels
    band = right_ref.shape[0] // channels
    count = len(blocks) * piece
    padded = blocks + [blocks[-1]] * (-len(blocks) % (fold // math.gcd(fold, piece)))
    left_blocks = jnp.concatenate(
        [b[x * piece * ROWS : (x + 1) * piece * ROWS, :] for x in range(fold) for b in blocks], axis=0
    )
    right_blocks = jnp.concatenate([b[half:, :] for b in padded], axis=0)
    size = count * band * ROWS
    for way, (rows, columns) in enumerate(((left_ref[...], right_blocks), (left_blocks, right_ref[...]))):
        product = lax.dot_general(rows, columns, NT, preferred_element_type=jnp.float32)
        inner = product.shape[0] // fold
        for n in range(0, product.shape[1], LANES):
            parts = [product[x * inner : (x + 1) * inner, n : n + LANES] for x in range(fold)]
            for m, part in enumerate(trade_chunks(parts, channels)):
                at = (n // channels + m) * inner
                if at < size:
                    scratch[way * size + at : way * size + at + inner, :] = part
    flat = jnp.concatenate(
        [scratch[pl.ds(g, 2 * band * count, stride=ROWS), :] for g in range(ROWS)], axis=1
    )
    high = flat.astype(jnp.bfloat16)
    low = (flat - high.astype(jnp.float32)).astype(jnp.bfloat16)
    ready()
    weight = jnp.concatenate(
        [
            weight_ref[(x * ROWS + g) * channels : (x * ROWS + g + 1) * channels, :]
            for g in range(ROWS)
            for x in range(fold)
        ],
        axis=0,
    )
    terms = jnp.dot(jnp.concatenate([high, low], axis=0), weight, preferred_element_type=jnp.float32)
    terms = terms[: 2 * band * count] + terms[2 * band * count :]
    scratch[: band * count, :] = terms[: band * count]
    for i in range(band):
        store(i, 0, scratch[pl.ds(i, count, stride=band), :])
        store(i, 1, terms[(band + i) * count : (band + i + 1) * count])


def early_kernel(dims, block_count, total, *refs):
    channels, _, sub_count = dims
    blocks, (left_ref, right_ref, other_ref), refs = refs[:block_count], refs[block_count:][:3], refs[block_count + 3 :]
    params = (len(refs) - 5) // 2
    sources, (terms_out, right_out), refs = refs[:params], refs[params:][:2], refs[params + 2 :]
    targets, (both, scratch, semaphores) = refs[:params], refs[params:]
    copies = fetch(sources, targets, semaphores)
    seqs = right_ref.shape[1]
    piece = right_ref.shape[0] // channels
    sub = lax.axis_index("sub")
    mine = row_in_tile(sub_count)
    both[sub] = right_ref[...].reshape(piece, channels, seqs)
    both[1 - sub] = other_ref[...].reshape(piece, channels, seqs)
    for i in range(right_out.shape[0] // channels):
        here = mine ^ i
        right_out[i * channels : (i + 1) * channels, :] = both[here // piece, here % piece]

    def store(i, way, terms):
        at = (i * 2 + way) * total
        terms_out[at : at + terms.shape[0], :] = terms

    pair_terms(channels, list(blocks), left_ref, right_out, targets[0], scratch, store, copies[0].wait)
    for copy in copies[1:]:
        copy.wait()


def late_kernel(dims, block_count, total, *refs):
    channels, depth_count, _ = dims
    blocks, (left_ref, right_ref, weight_ref, terms_ref) = refs[:block_count], refs[block_count : block_count + 4]
    keep_ref, core_ref, chip_ref, scratch = refs[block_count + 4 :]
    keep_ref[...] = terms_ref[: 2 * total, :]
    core_ref[...] = terms_ref[2 * total : 4 * total, :]
    if depth_count > 1:
        chip_ref[...] = terms_ref[4 * total :, :]

    def store(i, way, terms):
        target = (keep_ref, core_ref, chip_ref)[min(i, 2)]
        at = (max(i - 2, 0) * 2 + way + 1) * total
        target[at - terms.shape[0] : at, :] = terms

    pair_terms(channels, list(blocks), left_ref, right_ref, weight_ref, scratch, store, lambda: None)


def finish_kernel(
    dims,
    block_tiles,
    total_seqs,
    keep_ref,
    core_ref,
    chip_ref,
    relay_ref,
    out_bias,
    gate_weight,
    up_weight,
    down_weight,
    bins_weight,
    bins_bias,
    symmetric_out,
    bins_out,
):
    _, depth_count, sub_count = dims
    pair_channels = gate_weight.shape[0]
    bins = bins_weight.shape[0]
    count = keep_ref.shape[0] // 2
    piece = count // len(block_tiles)
    band = piece * sub_count
    tile, sub = lax.axis_index("tile"), lax.axis_index("sub")
    if depth_count > 1:
        here = keep_ref[...] + relay_ref[: 2 * count, :]
        there = core_ref[...] + chip_ref[2 * count :, :]
    else:
        here, there = keep_ref[...], core_ref[...]
    summed = jnp.concatenate([here[:count], there[:count], here[count:], there[count:]], axis=0)
    pair = (summed * (1.0 / total_seqs) + out_bias[...]).astype(jnp.bfloat16)
    values = pair.astype(jnp.float32)
    center = jnp.mean(values, axis=-1, keepdims=True)
    shifted = values - center
    spread = jnp.mean(shifted * shifted, axis=-1, keepdims=True)
    normed = (shifted * lax.rsqrt(spread + 1e-05)).astype(jnp.bfloat16)
    gate = jnp.dot(normed, gate_weight[...], preferred_element_type=jnp.float32)
    up = jnp.dot(normed, up_weight[...], preferred_element_type=jnp.float32)
    hidden = (jax.nn.silu(gate) * up).astype(jnp.bfloat16)
    moved = (values + jnp.dot(hidden, down_weight[...], preferred_element_type=jnp.float32)).astype(jnp.bfloat16)
    moved = moved.astype(jnp.float32)
    symmetric = ((moved[: 2 * count] + moved[2 * count :]) * 0.5).astype(jnp.bfloat16)
    packed = LANES // bins
    weight = jnp.concatenate([bins_weight[...]] * packed, axis=0)
    bias = jnp.concatenate([bins_bias[...]] * packed, axis=1)
    logits = lax.dot_general(symmetric, weight, NT, preferred_element_type=jnp.float32) + bias
    lane = lax.broadcasted_iota(jnp.int32, (1, LANES), 1)
    symmetric = symmetric.astype(jnp.float32)
    for side in range(2):
        for k, bits in enumerate(block_tiles):
            half = sub ^ (parity(bits) ^ side)
            start = (tile ^ bits) * band + half * piece
            row = side * count + k * piece
            for j in range(piece):
                at = pl.multiple_of((start + j) * pair_channels, pair_channels)
                symmetric_out[:, pl.ds(at, pair_channels)] = symmetric[row + j : row + j + 1].astype(jnp.bfloat16)
            for j in range(0, piece, packed):
                line = logits[row + j : row + j + 1]
                for p in range(1, packed):
                    line = jnp.where(lane < p * bins, line, logits[row + j + p : row + j + p + 1])
                at = pl.multiple_of((start + j) * bins, LANES)
                bins_out[:, pl.ds(at, LANES)] = line


def call(kernel, flops, outs, scratch, operands, sources=()):
    arrays = [(a.shape, a.dtype) for a in (*operands, *outs)]
    arrays += [(a.shape, a.dtype) for a in scratch if a.memory_space == pltpu.VMEM]
    size = sum(math.prod(dims) * jnp.dtype(kind).itemsize for dims, kind in arrays)
    return pl.pallas_call(
        kernel,
        out_shape=outs,
        in_specs=[VMEM] * len(operands) + [HBM] * len(sources),
        out_specs=(VMEM,) * len(outs),
        scratch_shapes=scratch,
        compiler_params=pltpu.CompilerParams(vmem_limit_bytes=min(2 * size + (2 << 20), 60 << 20)),
        cost_estimate=pl.CostEstimate(flops=flops, bytes_accessed=size, transcendentals=0),
    )(*operands, *(pltpu.with_memory_space_constraint(s, pltpu.HBM) for s in sources))


def shape(rows, columns, kind):
    return jax.ShapeDtypeStruct((rows, columns), kind)


def per_device(
    left_mantissa,
    left_exponent,
    right_mantissa,
    right_exponent,
    residue_mask,
    out_weight,
    out_bias,
    gate_weight,
    up_weight,
    down_weight,
    distogram_weight,
    distogram_bias,
):
    tile_count, depth_count, sub_count = (lax.axis_size(a) for a in GROUP)
    seqs, width = left_mantissa.shape
    band = left_exponent.shape[1]
    piece = right_exponent.shape[1]
    channels = width // band
    fold = channels // ROWS
    residues = residue_mask.shape[0]
    pair_channels = out_weight.shape[1]
    bins = distogram_weight.shape[1]
    if channels * fold != LANES or band % fold or sub_count != 2 or band != depth_count * sub_count or tile_count & (tile_count - 1) or band & (band - 1):
        raise ValueError("unsupported mesh")
    dims = (channels, depth_count, sub_count)
    bf16, f32 = jnp.bfloat16, jnp.float32

    sources = (left_mantissa, left_exponent.T, right_mantissa.T, right_exponent.T, residue_mask)
    own, left_rows, right_rows = call(
        functools.partial(prepare_kernel, dims),
        1 << 16,
        (
            shape(2 * piece * channels, seqs, bf16),
            shape(band * channels, seqs, bf16),
            shape(piece * channels, seqs, bf16),
        ),
        [pltpu.VMEM(s.shape, s.dtype) for s in sources[:4]]
        + [
            pltpu.SMEM(residue_mask.shape, residue_mask.dtype),
            pltpu.VMEM((band * channels, seqs), f32),
            pltpu.SemaphoreType.DMA((len(sources),)),
        ],
        (),
        sources,
    )
    blocks = {0: own}
    for bit in bits_of(tile_count):
        for bits in list(blocks):
            blocks[bits ^ bit] = xor_permute(blocks[bits], bit, 0, 1)
    other_rows = xor_permute(right_rows, 0, 0, 1)
    order = list(blocks)
    early, late = order[: max(len(order) * 3 // 4, 1)], order[max(len(order) * 3 // 4, 1) :]
    count = len(order) * piece
    params = (
        out_weight,
        out_bias.reshape(1, -1),
        gate_weight,
        up_weight,
        down_weight,
        distogram_weight.T,
        distogram_bias.reshape(1, -1),
    )
    terms, right_rows, weight, *params = call(
        functools.partial(early_kernel, dims, len(early), count),
        1 << 26,
        (
            shape(band * 2 * count, pair_channels, f32),
            shape(band * channels, seqs, bf16),
            *(shape(*p.shape, p.dtype) for p in params),
        ),
        [
            pltpu.VMEM((sub_count, piece, channels, seqs), bf16),
            pltpu.VMEM((2 * band * len(early) * piece * ROWS, LANES), f32),
            pltpu.SemaphoreType.DMA((len(params),)),
        ],
        (*(blocks[k] for k in early), left_rows, right_rows, other_rows),
        params,
    )
    keep, core, chip = call(
        functools.partial(late_kernel, dims, len(late), count),
        1 << 26,
        (
            shape(2 * count, pair_channels, f32),
            shape(2 * count, pair_channels, f32),
            shape(max(band - sub_count, 1) * 2 * count, pair_channels, f32),
        ),
        [pltpu.VMEM((2 * band * len(late) * piece * ROWS, LANES), f32)],
        (*(blocks[k] for k in late), left_rows, right_rows, weight, terms),
    )
    block_tiles = tuple(order)
    size = sub_count * 2 * count
    for bit in bits_of(depth_count)[:-1]:
        rows = jnp.concatenate([keep, core, chip], axis=0)
        rows = rows.reshape(-1, 2, bit, size // sub_count * sub_count, pair_channels)[0]
        mine = rows[0] + xor_permute(rows[1], 0, bit, 0)
        mine = mine.reshape(-1, pair_channels)
        keep, core, chip = mine[: size // 2], mine[size // 2 : size], mine[size:]
    from_chip = xor_permute(chip, 0, 1, 1) if depth_count > 1 else chip
    from_core = xor_permute(core, 0, 0, 1)
    relayed = xor_permute(from_chip[: 2 * count], 0, 0, 1) if depth_count > 1 else from_core
    return call(
        functools.partial(finish_kernel, dims, block_tiles, seqs * depth_count),
        1 << 25,
        (shape(1, residues * pair_channels, bf16), shape(1, residues * bins, f32)),
        [],
        (
            keep,
            from_core,
            from_chip,
            relayed,
            *params,
        ),
    )


def solution(mesh):
    in_specs = (
        P(("parts", "depth"), "tile"),
        P(("parts", "depth"), "tile"),
        P(("parts", "depth"), ("tile", "sub")),
        P(("parts", "depth"), ("tile", "sub")),
        P("parts"),
        P(),
        P(),
        P(),
        P(),
        P(),
        P(),
        P(),
    )
    out_specs = (
        P(("parts", "tile", "depth", "sub"), None),
        P(("parts", "tile", "depth", "sub"), None),
    )
    step = jax.shard_map(
        per_device, mesh=mesh, in_specs=in_specs, out_specs=out_specs, check_vma=False
    )
    known = [0]
    for bit in bits_of(mesh.shape["tile"]):
        for bits in list(known):
            known.append(bits ^ bit)
    return step
```

```python
import functools
import math

import jax
import jax.numpy as jnp
from jax import lax
from jax.experimental import pallas as pl
from jax.experimental.pallas import tpu as pltpu
from jax.sharding import PartitionSpec as P


LANES = 128
ROWS = 8
GROUP = ("tile", "depth", "sub")
NT = (((1,), (1,)), ((), ()))
VMEM = pl.BlockSpec(memory_space=pltpu.VMEM)
HBM = pl.BlockSpec(memory_space=pltpu.HBM)


def parity(number):
    return bin(number).count("1") & 1


def xor_permute(value, tile_bits, depth_bits, sub_bits):
    depth_count, sub_count = lax.axis_size("depth"), lax.axis_size("sub")
    pairs = []
    for t in range(lax.axis_size("tile")):
        for d in range(depth_count):
            for s in range(sub_count):
                here = (t * depth_count + d) * sub_count + s
                there = ((t ^ tile_bits) * depth_count + (d ^ depth_bits)) * sub_count + (s ^ sub_bits)
                pairs.append((here, there))
    return lax.ppermute(value, GROUP, pairs)


def bits_of(count):
    return [1 << b for b in reversed(range(count.bit_length() - 1))]


def row_in_tile(sub_count):
    return lax.axis_index("depth") * sub_count + lax.axis_index("sub")


def fetch(sources, targets, semaphores):
    copies = [
        pltpu.make_async_copy(source, target, semaphores.at[n])
        for n, (source, target) in enumerate(zip(sources, targets))
    ]
    for copy in copies:
        copy.start()
    return copies


def prepare_kernel(dims, *refs):
    channels, _, sub_count = dims
    sources, (block_ref, left_out, right_out), scratch = refs[:5], refs[5:8], refs[8:]
    left_ref, left_exp_ref, right_ref, right_exp_ref, mask_ref, left_f32, semaphores = scratch
    for copy in fetch(sources, scratch, semaphores):
        copy.wait()
    band = left_exp_ref.shape[0]
    piece = right_exp_ref.shape[0]
    fold = channels // ROWS
    tile, sub = lax.axis_index("tile"), lax.axis_index("sub")
    mine = row_in_tile(sub_count)
    half = fold * piece * ROWS
    right = right_ref[...].astype(jnp.float32)
    right_scale = jnp.exp2(right_exp_ref[...].astype(jnp.float32))
    first = tile * band + sub * piece
    for j in range(piece):
        scale = right_scale[j : j + 1] * mask_ref[first + j].astype(jnp.float32)
        scaled = (right[j * channels : (j + 1) * channels] * scale).astype(jnp.bfloat16)
        right_out[j * channels : (j + 1) * channels, :] = scaled
        block_ref[half + j * channels : half + (j + 1) * channels, :] = scaled
    left = jnp.transpose(left_ref[...].astype(jnp.float32))
    left_scale = jnp.exp2(left_exp_ref[...].astype(jnp.float32))
    for i in range(band):
        scale = left_scale[i : i + 1] * mask_ref[tile * band + i].astype(jnp.float32)
        left_f32[i * channels : (i + 1) * channels, :] = left[i * channels : (i + 1) * channels] * scale
    for target, places in (
        (block_ref, [sub * piece + j for j in range(piece)]),
        (left_out, [mine ^ i for i in range(band)]),
    ):
        for x in range(fold):
            rows = [
                left_f32[pl.ds(pl.multiple_of(place * channels + x * ROWS, ROWS), ROWS), :] for place in places
            ]
            at = x * len(places) * ROWS
            target[at : at + len(places) * ROWS, :] = jnp.concatenate(rows, axis=0).astype(jnp.bfloat16)


def pair_terms(channels, blocks, left_ref, right_ref, weight_ref, scratch, store, ready):
    fold = channels // ROWS
    piece = (blocks[0].shape[0] // channels) // 2
    half = piece * channels
    band = right_ref.shape[0] // channels
    count = len(blocks) * piece
    left_blocks = jnp.concatenate(
        [b[x * piece * ROWS : (x + 1) * piece * ROWS, :] for x in range(fold) for b in blocks], axis=0
    )
    right_blocks = jnp.concatenate([b[half:, :] for b in blocks], axis=0)
    chunk = lax.broadcasted_iota(jnp.int32, (1, LANES), 1) // channels
    size = count * band * ROWS
    for way, (rows, columns) in enumerate(((left_ref[...], right_blocks), (left_blocks, right_ref[...]))):
        members = range(columns.shape[0] // channels)
        wide = jnp.concatenate(
            [columns[m * channels : (m + 1) * channels] for m in members for _ in range(fold)], axis=0
        )
        product = lax.dot_general(rows, wide, NT, preferred_element_type=jnp.float32)
        inner = product.shape[0] // fold
        for m in members:
            lanes = slice(m * LANES, (m + 1) * LANES)
            value = product[:inner, lanes]
            for x in range(1, fold):
                value = jnp.where(chunk == x, product[x * inner : (x + 1) * inner, lanes], value)
            scratch[way * size + m * inner : way * size + (m + 1) * inner, :] = value
    flat = jnp.concatenate(
        [scratch[pl.ds(g, 2 * band * count, stride=ROWS), :] for g in range(ROWS)], axis=1
    )
    high = flat.astype(jnp.bfloat16)
    low = (flat - high.astype(jnp.float32)).astype(jnp.bfloat16)
    ready()
    weight = jnp.concatenate(
        [
            weight_ref[(x * ROWS + g) * channels : (x * ROWS + g + 1) * channels, :]
            for g in range(ROWS)
            for x in range(fold)
        ],
        axis=0,
    )
    terms = jnp.dot(jnp.concatenate([high, low], axis=0), weight, preferred_element_type=jnp.float32)
    terms = terms[: 2 * band * count] + terms[2 * band * count :]
    scratch[: band * count, :] = terms[: band * count]
    for i in range(band):
        store(i, 0, scratch[pl.ds(i, count, stride=band), :])
        store(i, 1, terms[(band + i) * count : (band + i + 1) * count])


def early_kernel(dims, block_count, total, *refs):
    channels, _, sub_count = dims
    blocks, (left_ref, right_ref, other_ref), refs = refs[:block_count], refs[block_count:][:3], refs[block_count + 3 :]
    params = (len(refs) - 5) // 2
    sources, (terms_out, right_out), refs = refs[:params], refs[params:][:2], refs[params + 2 :]
    targets, (both, scratch, semaphores) = refs[:params], refs[params:]
    copies = fetch(sources, targets, semaphores)
    seqs = right_ref.shape[1]
    piece = right_ref.shape[0] // channels
    sub = lax.axis_index("sub")
    mine = row_in_tile(sub_count)
    both[sub] = right_ref[...].reshape(piece, channels, seqs)
    both[1 - sub] = other_ref[...].reshape(piece, channels, seqs)
    for i in range(right_out.shape[0] // channels):
        here = mine ^ i
        right_out[i * channels : (i + 1) * channels, :] = both[here // piece, here % piece]

    def store(i, way, terms):
        at = (i * 2 + way) * total
        terms_out[at : at + terms.shape[0], :] = terms

    pair_terms(channels, list(blocks), left_ref, right_out, targets[0], scratch, store, copies[0].wait)
    for copy in copies[1:]:
        copy.wait()


def late_kernel(dims, block_count, total, *refs):
    channels, depth_count, _ = dims
    blocks, (left_ref, right_ref, weight_ref, terms_ref) = refs[:block_count], refs[block_count : block_count + 4]
    keep_ref, core_ref, chip_ref, scratch = refs[block_count + 4 :]
    keep_ref[...] = terms_ref[: 2 * total, :]
    core_ref[...] = terms_ref[2 * total : 4 * total, :]
    if depth_count > 1:
        chip_ref[...] = terms_ref[4 * total :, :]

    def store(i, way, terms):
        target = (keep_ref, core_ref, chip_ref)[min(i, 2)]
        at = (max(i - 2, 0) * 2 + way + 1) * total
        target[at - terms.shape[0] : at, :] = terms

    pair_terms(channels, list(blocks), left_ref, right_ref, weight_ref, scratch, store, lambda: None)


def half_row(total_seqs, summed, out_bias, gate_weight, up_weight, down_weight, bins_weight, bins_bias):
    count = summed.shape[0] // 2
    pair = (summed * (1.0 / total_seqs) + out_bias[...]).astype(jnp.bfloat16)
    values = pair.astype(jnp.float32)
    center = jnp.mean(values, axis=-1, keepdims=True)
    shifted = values - center
    spread = jnp.mean(shifted * shifted, axis=-1, keepdims=True)
    normed = (shifted * lax.rsqrt(spread + 1e-05)).astype(jnp.bfloat16)
    gate = jnp.dot(normed, gate_weight[...], preferred_element_type=jnp.float32)
    up = jnp.dot(normed, up_weight[...], preferred_element_type=jnp.float32)
    hidden = (jax.nn.silu(gate) * up).astype(jnp.bfloat16)
    moved = (values + jnp.dot(hidden, down_weight[...], preferred_element_type=jnp.float32)).astype(jnp.bfloat16)
    moved = moved.astype(jnp.float32)
    symmetric = ((moved[:count] + moved[count:]) * 0.5).astype(jnp.bfloat16)
    packed = LANES // bins_weight.shape[0]
    weight = jnp.concatenate([bins_weight[...]] * packed, axis=0)
    bias = jnp.concatenate([bins_bias[...]] * packed, axis=1)
    logits = lax.dot_general(symmetric, weight, NT, preferred_element_type=jnp.float32) + bias
    return symmetric.astype(jnp.float32), logits


def there_kernel(total_seqs, depth_count, core_ref, chip_ref, *refs):
    params, (symmetric_out, logits_out) = refs[:-2], refs[-2:]
    summed = core_ref[...]
    if depth_count > 1:
        summed = summed + chip_ref[summed.shape[0] :, :]
    symmetric_out[...], logits_out[...] = half_row(total_seqs, summed, *params)


def here_kernel(dims, block_tiles, total_seqs, keep_ref, relay_ref, symmetric_there, logits_there, *refs):
    _, depth_count, sub_count = dims
    params, (symmetric_out, bins_out) = refs[:-2], refs[-2:]
    count, pair_channels = symmetric_there.shape
    bins = params[-2].shape[0]
    piece = count // len(block_tiles)
    band = piece * sub_count
    packed = LANES // bins
    tile, sub = lax.axis_index("tile"), lax.axis_index("sub")
    lane = lax.broadcasted_iota(jnp.int32, (1, LANES), 1)

    def write(side, symmetric, logits):
        for k, bits in enumerate(block_tiles):
            half = sub ^ (parity(bits) ^ side)
            start = (tile ^ bits) * band + half * piece
            row = k * piece
            for j in range(piece):
                at = pl.multiple_of((start + j) * pair_channels, pair_channels)
                symmetric_out[:, pl.ds(at, pair_channels)] = symmetric[row + j : row + j + 1].astype(jnp.bfloat16)
            for j in range(0, piece, packed):
                line = logits[row + j : row + j + 1]
                for p in range(1, packed):
                    line = jnp.where(lane < p * bins, line, logits[row + j + p : row + j + p + 1])
                at = pl.multiple_of((start + j) * bins, LANES)
                bins_out[:, pl.ds(at, LANES)] = line

    write(1, symmetric_there[...], logits_there[...])
    summed = keep_ref[...]
    if depth_count > 1:
        summed = summed + relay_ref[...]
    write(0, *half_row(total_seqs, summed, *params))


def call(kernel, flops, outs, scratch, operands, sources=()):
    arrays = [(a.shape, a.dtype) for a in (*operands, *outs)]
    arrays += [(a.shape, a.dtype) for a in scratch if a.memory_space == pltpu.VMEM]
    size = sum(math.prod(dims) * jnp.dtype(kind).itemsize for dims, kind in arrays)
    return pl.pallas_call(
        kernel,
        out_shape=outs,
        in_specs=[VMEM] * len(operands) + [HBM] * len(sources),
        out_specs=(VMEM,) * len(outs),
        scratch_shapes=scratch,
        compiler_params=pltpu.CompilerParams(vmem_limit_bytes=min(2 * size + (2 << 20), 60 << 20)),
        cost_estimate=pl.CostEstimate(flops=flops, bytes_accessed=size, transcendentals=0),
    )(*operands, *(pltpu.with_memory_space_constraint(s, pltpu.HBM) for s in sources))


def shape(rows, columns, kind):
    return jax.ShapeDtypeStruct((rows, columns), kind)


def per_device(
    left_mantissa,
    left_exponent,
    right_mantissa,
    right_exponent,
    residue_mask,
    out_weight,
    out_bias,
    gate_weight,
    up_weight,
    down_weight,
    distogram_weight,
    distogram_bias,
):
    tile_count, depth_count, sub_count = (lax.axis_size(a) for a in GROUP)
    seqs, width = left_mantissa.shape
    band = left_exponent.shape[1]
    piece = right_exponent.shape[1]
    channels = width // band
    fold = channels // ROWS
    residues = residue_mask.shape[0]
    pair_channels = out_weight.shape[1]
    bins = distogram_weight.shape[1]
    if channels * fold != LANES or piece * bins % LANES or sub_count != 2 or band != depth_count * sub_count or tile_count & (tile_count - 1) or band & (band - 1):
        raise ValueError("unsupported mesh")
    dims = (channels, depth_count, sub_count)
    bf16, f32 = jnp.bfloat16, jnp.float32

    sources = (left_mantissa, left_exponent.T, right_mantissa.T, right_exponent.T, residue_mask)
    own, left_rows, right_rows = call(
        functools.partial(prepare_kernel, dims),
        1 << 16,
        (
            shape(2 * piece * channels, seqs, bf16),
            shape(band * channels, seqs, bf16),
            shape(piece * channels, seqs, bf16),
        ),
        [pltpu.VMEM(s.shape, s.dtype) for s in sources[:4]]
        + [
            pltpu.SMEM(residue_mask.shape, residue_mask.dtype),
            pltpu.VMEM((band * channels, seqs), f32),
            pltpu.SemaphoreType.DMA((len(sources),)),
        ],
        (),
        sources,
    )
    blocks = {0: own}
    for bit in bits_of(tile_count):
        for bits in list(blocks):
            blocks[bits ^ bit] = xor_permute(blocks[bits], bit, 0, 1)
    other_rows = xor_permute(right_rows, 0, 0, 1)
    order = list(blocks)
    early, late = order[: max(len(order) * 3 // 4, 1)], order[max(len(order) * 3 // 4, 1) :]
    count = len(order) * piece
    params = (
        out_weight,
        out_bias.reshape(1, -1),
        gate_weight,
        up_weight,
        down_weight,
        distogram_weight.T,
        distogram_bias.reshape(1, -1),
    )
    terms, right_rows, weight, *params = call(
        functools.partial(early_kernel, dims, len(early), count),
        1 << 26,
        (
            shape(band * 2 * count, pair_channels, f32),
            shape(band * channels, seqs, bf16),
            *(shape(*p.shape, p.dtype) for p in params),
        ),
        [
            pltpu.VMEM((sub_count, piece, channels, seqs), bf16),
            pltpu.VMEM((2 * band * len(early) * piece * ROWS, LANES), f32),
            pltpu.SemaphoreType.DMA((len(params),)),
        ],
        (*(blocks[k] for k in early), left_rows, right_rows, other_rows),
        params,
    )
    keep, core, chip = call(
        functools.partial(late_kernel, dims, len(late), count),
        1 << 26,
        (
            shape(2 * count, pair_channels, f32),
            shape(2 * count, pair_channels, f32),
            shape(max(band - sub_count, 1) * 2 * count, pair_channels, f32),
        ),
        [pltpu.VMEM((2 * band * len(late) * piece * ROWS, LANES), f32)],
        (*(blocks[k] for k in late), left_rows, right_rows, weight, terms),
    )
    block_tiles = tuple(order)
    size = sub_count * 2 * count
    for bit in bits_of(depth_count)[:-1]:
        rows = jnp.concatenate([keep, core, chip], axis=0)
        rows = rows.reshape(-1, 2, bit, size // sub_count * sub_count, pair_channels)[0]
        mine = rows[0] + xor_permute(rows[1], 0, bit, 0)
        mine = mine.reshape(-1, pair_channels)
        keep, core, chip = mine[: size // 2], mine[size // 2 : size], mine[size:]
    from_chip = xor_permute(chip, 0, 1, 1) if depth_count > 1 else chip
    from_core = xor_permute(core, 0, 0, 1)
    relayed = xor_permute(from_chip[: 2 * count], 0, 0, 1) if depth_count > 1 else from_core
    total_seqs = seqs * depth_count
    there = call(
        functools.partial(there_kernel, total_seqs, depth_count),
        1 << 24,
        (shape(count, pair_channels, f32), shape(count, LANES, f32)),
        [],
        (from_core, from_chip, *params),
    )
    return call(
        functools.partial(here_kernel, dims, block_tiles, total_seqs),
        1 << 24,
        (shape(1, residues * pair_channels, bf16), shape(1, residues * bins, f32)),
        [],
        (keep, relayed, *there, *params),
    )


def solution(mesh):
    in_specs = (
        P(("parts", "depth"), "tile"),
        P(("parts", "depth"), "tile"),
        P(("parts", "depth"), ("tile", "sub")),
        P(("parts", "depth"), ("tile", "sub")),
        P("parts"),
        P(),
        P(),
        P(),
        P(),
        P(),
        P(),
        P(),
    )
    out_specs = (
        P(("parts", "tile", "depth", "sub"), None),
        P(("parts", "tile", "depth", "sub"), None),
    )
    step = jax.shard_map(
        per_device, mesh=mesh, in_specs=in_specs, out_specs=out_specs, check_vma=False
    )
    known = [0]
    for bit in bits_of(mesh.shape["tile"]):
        for bits in list(known):
            known.append(bits ^ bit)
    return step
```

```python
import functools
import math

import jax
import jax.numpy as jnp
from jax import lax
from jax.experimental import pallas as pl
from jax.experimental.pallas import tpu as pltpu
from jax.sharding import PartitionSpec as P


LANES = 128
ROWS = 8
GROUP = ("tile", "depth", "sub")
NT = (((1,), (1,)), ((), ()))
VMEM = pl.BlockSpec(memory_space=pltpu.VMEM)
HBM = pl.BlockSpec(memory_space=pltpu.HBM)


def parity(number):
    return bin(number).count("1") & 1


def xor_permute(value, tile_bits, depth_bits, sub_bits):
    depth_count, sub_count = lax.axis_size("depth"), lax.axis_size("sub")
    pairs = []
    for t in range(lax.axis_size("tile")):
        for d in range(depth_count):
            for s in range(sub_count):
                here = (t * depth_count + d) * sub_count + s
                there = ((t ^ tile_bits) * depth_count + (d ^ depth_bits)) * sub_count + (s ^ sub_bits)
                pairs.append((here, there))
    return lax.ppermute(value, GROUP, pairs)


def bits_of(count):
    return [1 << b for b in reversed(range(count.bit_length() - 1))]


def row_in_tile(sub_count):
    return lax.axis_index("depth") * sub_count + lax.axis_index("sub")


def fetch(sources, targets, semaphores):
    copies = [
        pltpu.make_async_copy(source, target, semaphores.at[n])
        for n, (source, target) in enumerate(zip(sources, targets))
    ]
    for copy in copies:
        copy.start()
    return copies


def prepare_kernel(*refs):
    sources, block_ref, scratch = refs[:5], refs[5], refs[6:]
    left_ref, left_exp_ref, right_ref, right_exp_ref, mask_ref, turned, semaphores = scratch
    for copy in fetch(sources, scratch, semaphores):
        copy.wait()
    band = left_exp_ref.shape[0]
    piece = right_exp_ref.shape[0]
    channels = right_ref.shape[0] // piece
    sub = lax.axis_index("sub")
    first = lax.axis_index("tile") * band + sub * piece
    turned[...] = jnp.transpose(left_ref[...])
    for j in range(piece):
        keep = mask_ref[first + j].astype(jnp.float32)
        scale = jnp.exp2(right_exp_ref[j : j + 1].astype(jnp.float32)) * keep
        right = right_ref[j * channels : (j + 1) * channels].astype(jnp.float32) * scale
        block_ref[(piece + j) * channels : (piece + j + 1) * channels, :] = right.astype(jnp.bfloat16)
        place = sub * piece + j
        scale = jnp.exp2(left_exp_ref[pl.ds(place, 1), :].astype(jnp.float32)) * keep
        rows = turned[pl.ds(pl.multiple_of(place * channels, channels), channels), :]
        left = (rows.astype(jnp.float32) * scale).astype(jnp.bfloat16)
        for x in range(channels // ROWS):
            at = (x * piece + j) * ROWS
            block_ref[at : at + ROWS, :] = left[x * ROWS : (x + 1) * ROWS]


def pair_terms(channels, blocks, left_ref, right_ref, weight_ref, scratch, store, ready):
    fold = channels // ROWS
    piece = (blocks[0].shape[0] // channels) // 2
    half = piece * channels
    band = right_ref.shape[0] // channels
    count = len(blocks) * piece
    left_blocks = jnp.concatenate(
        [b[x * piece * ROWS : (x + 1) * piece * ROWS, :] for x in range(fold) for b in blocks], axis=0
    )
    right_blocks = jnp.concatenate([b[half:, :] for b in blocks], axis=0)
    chunk = lax.broadcasted_iota(jnp.int32, (1, LANES), 1) // channels
    size = count * band * ROWS
    for way, (rows, columns) in enumerate(((left_ref[...], right_blocks), (left_blocks, right_ref[...]))):
        members = range(columns.shape[0] // channels)
        wide = jnp.concatenate(
            [columns[m * channels : (m + 1) * channels] for m in members for _ in range(fold)], axis=0
        )
        product = lax.dot_general(rows, wide, NT, preferred_element_type=jnp.float32)
        inner = product.shape[0] // fold
        for m in members:
            lanes = slice(m * LANES, (m + 1) * LANES)
            value = product[:inner, lanes]
            for x in range(1, fold):
                value = jnp.where(chunk == x, product[x * inner : (x + 1) * inner, lanes], value)
            scratch[way * size + m * inner : way * size + (m + 1) * inner, :] = value
    flat = jnp.concatenate(
        [scratch[pl.ds(g, 2 * band * count, stride=ROWS), :] for g in range(ROWS)], axis=1
    )
    high = flat.astype(jnp.bfloat16)
    low = (flat - high.astype(jnp.float32)).astype(jnp.bfloat16)
    ready()
    weight = jnp.concatenate(
        [
            weight_ref[(x * ROWS + g) * channels : (x * ROWS + g + 1) * channels, :]
            for g in range(ROWS)
            for x in range(fold)
        ],
        axis=0,
    )
    terms = jnp.dot(jnp.concatenate([high, low], axis=0), weight, preferred_element_type=jnp.float32)
    terms = terms[: 2 * band * count] + terms[2 * band * count :]
    scratch[: band * count, :] = terms[: band * count]
    for i in range(band):
        store(i, 0, scratch[pl.ds(i, count, stride=band), :])
        store(i, 1, terms[(band + i) * count : (band + i + 1) * count])


def early_kernel(dims, block_count, total, *refs):
    channels, _, sub_count = dims
    blocks, other_ref, refs = refs[:block_count], refs[block_count], refs[block_count + 1 :]
    params = (len(refs) - 7) // 2
    sources, (terms_out, left_out, right_out), refs = refs[:params], refs[params:][:3], refs[params + 3 :]
    targets, (left_both, right_both, scratch, semaphores) = refs[:params], refs[params:]
    copies = fetch(sources, targets, semaphores)
    seqs = other_ref.shape[1]
    fold = channels // ROWS
    piece = other_ref.shape[0] // channels // 2
    half = piece * channels
    band = right_out.shape[0] // channels
    sub = lax.axis_index("sub")
    mine = row_in_tile(sub_count)
    for place, block in ((sub, blocks[0]), (1 - sub, other_ref)):
        left_both[place] = block[:half, :].reshape(fold, piece, ROWS, seqs)
        right_both[place] = block[half:, :].reshape(piece, channels, seqs)
    for i in range(band):
        side, j = (mine ^ i) // piece, (mine ^ i) % piece
        right_out[i * channels : (i + 1) * channels, :] = right_both[side, j]
        for x in range(fold):
            at = (x * band + i) * ROWS
            left_out[at : at + ROWS, :] = left_both[side, x, j]

    def store(i, way, terms):
        at = (i * 2 + way) * total
        terms_out[at : at + terms.shape[0], :] = terms

    pair_terms(channels, list(blocks), left_out, right_out, targets[0], scratch, store, copies[0].wait)
    for copy in copies[1:]:
        copy.wait()


def late_kernel(dims, block_count, total, *refs):
    channels, depth_count, _ = dims
    blocks, (left_ref, right_ref, weight_ref, terms_ref) = refs[:block_count], refs[block_count : block_count + 4]
    keep_ref, core_ref, chip_ref, scratch = refs[block_count + 4 :]
    keep_ref[...] = terms_ref[: 2 * total, :]
    core_ref[...] = terms_ref[2 * total : 4 * total, :]
    if depth_count > 1:
        chip_ref[...] = terms_ref[4 * total :, :]

    def store(i, way, terms):
        target = (keep_ref, core_ref, chip_ref)[min(i, 2)]
        at = (max(i - 2, 0) * 2 + way + 1) * total
        target[at - terms.shape[0] : at, :] = terms

    pair_terms(channels, list(blocks), left_ref, right_ref, weight_ref, scratch, store, lambda: None)


def half_row(total_seqs, summed, out_bias, gate_weight, up_weight, down_weight, bins_weight, bins_bias):
    count = summed.shape[0] // 2
    pair = (summed * (1.0 / total_seqs) + out_bias[...]).astype(jnp.bfloat16)
    values = pair.astype(jnp.float32)
    center = jnp.mean(values, axis=-1, keepdims=True)
    shifted = values - center
    spread = jnp.mean(shifted * shifted, axis=-1, keepdims=True)
    normed = (shifted * lax.rsqrt(spread + 1e-05)).astype(jnp.bfloat16)
    gate = jnp.dot(normed, gate_weight[...], preferred_element_type=jnp.float32)
    up = jnp.dot(normed, up_weight[...], preferred_element_type=jnp.float32)
    hidden = (jax.nn.silu(gate) * up).astype(jnp.bfloat16)
    moved = (values + jnp.dot(hidden, down_weight[...], preferred_element_type=jnp.float32)).astype(jnp.bfloat16)
    moved = moved.astype(jnp.float32)
    symmetric = ((moved[:count] + moved[count:]) * 0.5).astype(jnp.bfloat16)
    packed = LANES // bins_weight.shape[0]
    weight = jnp.concatenate([bins_weight[...]] * packed, axis=0)
    bias = jnp.concatenate([bins_bias[...]] * packed, axis=1)
    logits = lax.dot_general(symmetric, weight, NT, preferred_element_type=jnp.float32) + bias
    return symmetric.astype(jnp.float32), logits


def there_kernel(total_seqs, depth_count, core_ref, chip_ref, *refs):
    params, (symmetric_out, logits_out) = refs[:-2], refs[-2:]
    summed = core_ref[...]
    if depth_count > 1:
        summed = summed + chip_ref[summed.shape[0] :, :]
    symmetric_out[...], logits_out[...] = half_row(total_seqs, summed, *params)


def here_kernel(dims, block_tiles, total_seqs, keep_ref, relay_ref, symmetric_there, logits_there, *refs):
    _, depth_count, sub_count = dims
    params, (symmetric_out, bins_out) = refs[:-2], refs[-2:]
    count, pair_channels = symmetric_there.shape
    bins = params[-2].shape[0]
    piece = count // len(block_tiles)
    band = piece * sub_count
    packed = LANES // bins
    tile, sub = lax.axis_index("tile"), lax.axis_index("sub")
    lane = lax.broadcasted_iota(jnp.int32, (1, LANES), 1)

    def write(side, symmetric, logits):
        for k, bits in enumerate(block_tiles):
            half = sub ^ (parity(bits) ^ side)
            start = (tile ^ bits) * band + half * piece
            row = k * piece
            for j in range(piece):
                at = pl.multiple_of((start + j) * pair_channels, pair_channels)
                symmetric_out[:, pl.ds(at, pair_channels)] = symmetric[row + j : row + j + 1].astype(jnp.bfloat16)
            for j in range(0, piece, packed):
                line = logits[row + j : row + j + 1]
                for p in range(1, packed):
                    line = jnp.where(lane < p * bins, line, logits[row + j + p : row + j + p + 1])
                at = pl.multiple_of((start + j) * bins, LANES)
                bins_out[:, pl.ds(at, LANES)] = line

    write(1, symmetric_there[...], logits_there[...])
    summed = keep_ref[...]
    if depth_count > 1:
        summed = summed + relay_ref[...]
    write(0, *half_row(total_seqs, summed, *params))


def call(kernel, flops, outs, scratch, operands, sources=()):
    arrays = [(a.shape, a.dtype) for a in (*operands, *outs)]
    arrays += [(a.shape, a.dtype) for a in scratch if a.memory_space == pltpu.VMEM]
    size = sum(math.prod(dims) * jnp.dtype(kind).itemsize for dims, kind in arrays)
    return pl.pallas_call(
        kernel,
        out_shape=outs,
        in_specs=[VMEM] * len(operands) + [HBM] * len(sources),
        out_specs=(VMEM,) * len(outs),
        scratch_shapes=scratch,
        compiler_params=pltpu.CompilerParams(vmem_limit_bytes=min(2 * size + (2 << 20), 60 << 20)),
        cost_estimate=pl.CostEstimate(flops=flops, bytes_accessed=size, transcendentals=0),
    )(*operands, *(pltpu.with_memory_space_constraint(s, pltpu.HBM) for s in sources))


def shape(rows, columns, kind):
    return jax.ShapeDtypeStruct((rows, columns), kind)


def per_device(
    left_mantissa,
    left_exponent,
    right_mantissa,
    right_exponent,
    residue_mask,
    out_weight,
    out_bias,
    gate_weight,
    up_weight,
    down_weight,
    distogram_weight,
    distogram_bias,
):
    tile_count, depth_count, sub_count = (lax.axis_size(a) for a in GROUP)
    seqs, width = left_mantissa.shape
    band = left_exponent.shape[1]
    piece = right_exponent.shape[1]
    channels = width // band
    fold = channels // ROWS
    residues = residue_mask.shape[0]
    pair_channels = out_weight.shape[1]
    bins = distogram_weight.shape[1]
    if channels * fold != LANES or piece * bins % LANES or sub_count != 2 or band != depth_count * sub_count or tile_count & (tile_count - 1) or band & (band - 1):
        raise ValueError("unsupported mesh")
    dims = (channels, depth_count, sub_count)
    bf16, f32 = jnp.bfloat16, jnp.float32

    sources = (left_mantissa, left_exponent.T, right_mantissa.T, right_exponent.T, residue_mask)
    (own,) = call(
        prepare_kernel,
        1 << 16,
        (shape(2 * piece * channels, seqs, bf16),),
        [pltpu.VMEM(s.shape, s.dtype) for s in sources[:4]]
        + [
            pltpu.SMEM(residue_mask.shape, residue_mask.dtype),
            pltpu.VMEM((width, seqs), bf16),
            pltpu.SemaphoreType.DMA((len(sources),)),
        ],
        (),
        sources,
    )
    blocks = {0: own}
    for bit in bits_of(tile_count):
        for bits in list(blocks):
            blocks[bits ^ bit] = xor_permute(blocks[bits], bit, 0, 1)
    other = xor_permute(own, 0, 0, 1)
    order = list(blocks)
    early, late = order[: max(len(order) * 3 // 4, 1)], order[max(len(order) * 3 // 4, 1) :]
    count = len(order) * piece
    params = (
        out_weight,
        out_bias.reshape(1, -1),
        gate_weight,
        up_weight,
        down_weight,
        distogram_weight.T,
        distogram_bias.reshape(1, -1),
    )
    terms, left_rows, right_rows, weight, *params = call(
        functools.partial(early_kernel, dims, len(early), count),
        1 << 26,
        (
            shape(band * 2 * count, pair_channels, f32),
            shape(band * channels, seqs, bf16),
            shape(band * channels, seqs, bf16),
            *(shape(*p.shape, p.dtype) for p in params),
        ),
        [
            pltpu.VMEM((sub_count, fold, piece, ROWS, seqs), bf16),
            pltpu.VMEM((sub_count, piece, channels, seqs), bf16),
            pltpu.VMEM((2 * band * len(early) * piece * ROWS, LANES), f32),
            pltpu.SemaphoreType.DMA((len(params),)),
        ],
        (*(blocks[k] for k in early), other),
        params,
    )
    keep, core, chip = call(
        functools.partial(late_kernel, dims, len(late), count),
        1 << 26,
        (
            shape(2 * count, pair_channels, f32),
            shape(2 * count, pair_channels, f32),
            shape(max(band - sub_count, 1) * 2 * count, pair_channels, f32),
        ),
        [pltpu.VMEM((2 * band * len(late) * piece * ROWS, LANES), f32)],
        (*(blocks[k] for k in late), left_rows, right_rows, weight, terms),
    )
    block_tiles = tuple(order)
    size = sub_count * 2 * count
    for bit in bits_of(depth_count)[:-1]:
        rows = jnp.concatenate([keep, core, chip], axis=0)
        rows = rows.reshape(-1, 2, bit, size // sub_count * sub_count, pair_channels)[0]
        mine = rows[0] + xor_permute(rows[1], 0, bit, 0)
        mine = mine.reshape(-1, pair_channels)
        keep, core, chip = mine[: size // 2], mine[size // 2 : size], mine[size:]
    from_chip = xor_permute(chip, 0, 1, 1) if depth_count > 1 else chip
    from_core = xor_permute(core, 0, 0, 1)
    relayed = xor_permute(from_chip[: 2 * count], 0, 0, 1) if depth_count > 1 else from_core
    total_seqs = seqs * depth_count
    there = call(
        functools.partial(there_kernel, total_seqs, depth_count),
        1 << 24,
        (shape(count, pair_channels, f32), shape(count, LANES, f32)),
        [],
        (from_core, from_chip, *params),
    )
    return call(
        functools.partial(here_kernel, dims, block_tiles, total_seqs),
        1 << 24,
        (shape(1, residues * pair_channels, bf16), shape(1, residues * bins, f32)),
        [],
        (keep, relayed, *there, *params),
    )


def solution(mesh):
    in_specs = (
        P(("parts", "depth"), "tile"),
        P(("parts", "depth"), "tile"),
        P(("parts", "depth"), ("tile", "sub")),
        P(("parts", "depth"), ("tile", "sub")),
        P("parts"),
        P(),
        P(),
        P(),
        P(),
        P(),
        P(),
        P(),
    )
    out_specs = (
        P(("parts", "tile", "depth", "sub"), None),
        P(("parts", "tile", "depth", "sub"), None),
    )
    step = jax.shard_map(
        per_device, mesh=mesh, in_specs=in_specs, out_specs=out_specs, check_vma=False
    )
    known = [0]
    for bit in bits_of(mesh.shape["tile"]):
        for bits in list(known):
            known.append(bits ^ bit)
    return step
```

```python
import functools
import math

import jax
import jax.numpy as jnp
from jax import lax
from jax.experimental import pallas as pl
from jax.experimental.pallas import tpu as pltpu
from jax.sharding import PartitionSpec as P


LANES = 128
ROWS = 8
GROUP = ("tile", "depth", "sub")
NT = (((1,), (1,)), ((), ()))
VMEM = pl.BlockSpec(memory_space=pltpu.VMEM)
HBM = pl.BlockSpec(memory_space=pltpu.HBM)


def parity(number):
    return bin(number).count("1") & 1


def xor_permute(value, tile_bits, depth_bits, sub_bits):
    depth_count, sub_count = lax.axis_size("depth"), lax.axis_size("sub")
    pairs = []
    for t in range(lax.axis_size("tile")):
        for d in range(depth_count):
            for s in range(sub_count):
                here = (t * depth_count + d) * sub_count + s
                there = ((t ^ tile_bits) * depth_count + (d ^ depth_bits)) * sub_count + (s ^ sub_bits)
                pairs.append((here, there))
    return lax.ppermute(value, GROUP, pairs)


def bits_of(count):
    return [1 << b for b in reversed(range(count.bit_length() - 1))]


def row_in_tile(sub_count):
    return lax.axis_index("depth") * sub_count + lax.axis_index("sub")


def fetch(sources, targets, semaphores):
    last = semaphores.shape[0] - 1
    copies = [
        pltpu.make_async_copy(source, target, semaphores.at[min(n, last)])
        for n, (source, target) in enumerate(zip(sources, targets))
    ]
    for copy in copies:
        copy.start()
    return copies


def prepare_kernel(*refs):
    sources, block_ref, scratch = refs[:5], refs[5], refs[6:]
    left_ref, left_exp_ref, right_ref, right_exp_ref, mask_ref, turned, semaphores = scratch
    for copy in fetch(sources, scratch, semaphores):
        copy.wait()
    band = left_exp_ref.shape[0]
    piece = right_exp_ref.shape[0]
    channels = right_ref.shape[0] // piece
    sub = lax.axis_index("sub")
    first = lax.axis_index("tile") * band + sub * piece
    turned[...] = jnp.transpose(left_ref[...])
    for j in range(piece):
        keep = mask_ref[first + j].astype(jnp.float32)
        scale = jnp.exp2(right_exp_ref[j : j + 1].astype(jnp.float32)) * keep
        right = right_ref[j * channels : (j + 1) * channels].astype(jnp.float32) * scale
        block_ref[(piece + j) * channels : (piece + j + 1) * channels, :] = right.astype(jnp.bfloat16)
        place = sub * piece + j
        scale = jnp.exp2(left_exp_ref[pl.ds(place, 1), :].astype(jnp.float32)) * keep
        rows = turned[pl.ds(pl.multiple_of(place * channels, channels), channels), :]
        left = (rows.astype(jnp.float32) * scale).astype(jnp.bfloat16)
        for x in range(channels // ROWS):
            at = (x * piece + j) * ROWS
            block_ref[at : at + ROWS, :] = left[x * ROWS : (x + 1) * ROWS]


def pair_terms(channels, blocks, left_ref, right_ref, weight_ref, scratch, store, ready):
    fold = channels // ROWS
    piece = (blocks[0].shape[0] // channels) // 2
    half = piece * channels
    band = right_ref.shape[0] // channels
    count = len(blocks) * piece
    left_blocks = jnp.concatenate(
        [b[x * piece * ROWS : (x + 1) * piece * ROWS, :] for x in range(fold) for b in blocks], axis=0
    )
    right_blocks = jnp.concatenate([b[half:, :] for b in blocks], axis=0)
    chunk = lax.broadcasted_iota(jnp.int32, (1, LANES), 1) // channels
    size = count * band * ROWS
    for way, (rows, columns) in enumerate(((left_ref[...], right_blocks), (left_blocks, right_ref[...]))):
        members = range(columns.shape[0] // channels)
        wide = jnp.concatenate(
            [columns[m * channels : (m + 1) * channels] for m in members for _ in range(fold)], axis=0
        )
        product = lax.dot_general(rows, wide, NT, preferred_element_type=jnp.float32)
        inner = product.shape[0] // fold
        for m in members:
            lanes = slice(m * LANES, (m + 1) * LANES)
            value = product[:inner, lanes]
            for x in range(1, fold):
                value = jnp.where(chunk == x, product[x * inner : (x + 1) * inner, lanes], value)
            scratch[way * size + m * inner : way * size + (m + 1) * inner, :] = value
    flat = jnp.concatenate(
        [scratch[pl.ds(g, 2 * band * count, stride=ROWS), :] for g in range(ROWS)], axis=1
    )
    high = flat.astype(jnp.bfloat16)
    low = (flat - high.astype(jnp.float32)).astype(jnp.bfloat16)
    ready()
    weight = jnp.concatenate(
        [
            weight_ref[(x * ROWS + g) * channels : (x * ROWS + g + 1) * channels, :]
            for g in range(ROWS)
            for x in range(fold)
        ],
        axis=0,
    )
    terms = jnp.dot(jnp.concatenate([high, low], axis=0), weight, preferred_element_type=jnp.float32)
    terms = terms[: 2 * band * count] + terms[2 * band * count :]
    scratch[: band * count, :] = terms[: band * count]
    for i in range(band):
        store(i, 0, scratch[pl.ds(i, count, stride=band), :])
        store(i, 1, terms[(band + i) * count : (band + i + 1) * count])


def early_kernel(dims, block_count, total, *refs):
    channels, _, sub_count = dims
    blocks, other_ref, refs = refs[:block_count], refs[block_count], refs[block_count + 1 :]
    params = (len(refs) - 7) // 2
    sources, (terms_out, left_out, right_out), refs = refs[:params], refs[params:][:3], refs[params + 3 :]
    targets, (left_both, right_both, scratch, semaphores) = refs[:params], refs[params:]
    copies = fetch(sources, targets, semaphores)
    seqs = other_ref.shape[1]
    fold = channels // ROWS
    piece = other_ref.shape[0] // channels // 2
    half = piece * channels
    band = right_out.shape[0] // channels
    sub = lax.axis_index("sub")
    mine = row_in_tile(sub_count)
    for place, block in ((sub, blocks[0]), (1 - sub, other_ref)):
        left_both[place] = block[:half, :].reshape(fold, piece, ROWS, seqs)
        right_both[place] = block[half:, :].reshape(piece, channels, seqs)
    for i in range(band):
        side, j = (mine ^ i) // piece, (mine ^ i) % piece
        right_out[i * channels : (i + 1) * channels, :] = right_both[side, j]
        for x in range(fold):
            at = (x * band + i) * ROWS
            left_out[at : at + ROWS, :] = left_both[side, x, j]

    def store(i, way, terms):
        at = (i * 2 + way) * total
        terms_out[at : at + terms.shape[0], :] = terms

    pair_terms(channels, list(blocks), left_out, right_out, targets[0], scratch, store, copies[0].wait)
    for copy in copies[1:]:
        copy.wait()


def late_kernel(dims, block_count, total, *refs):
    channels, depth_count, _ = dims
    blocks, (left_ref, right_ref, weight_ref, terms_ref) = refs[:block_count], refs[block_count : block_count + 4]
    keep_ref, core_ref, chip_ref, scratch = refs[block_count + 4 :]
    keep_ref[...] = terms_ref[: 2 * total, :]
    core_ref[...] = terms_ref[2 * total : 4 * total, :]
    if depth_count > 1:
        chip_ref[...] = terms_ref[4 * total :, :]

    def store(i, way, terms):
        target = (keep_ref, core_ref, chip_ref)[min(i, 2)]
        at = (max(i - 2, 0) * 2 + way + 1) * total
        target[at - terms.shape[0] : at, :] = terms

    pair_terms(channels, list(blocks), left_ref, right_ref, weight_ref, scratch, store, lambda: None)


def half_row(total_seqs, summed, out_bias, gate_weight, up_weight, down_weight, bins_weight, bins_bias):
    count = summed.shape[0] // 2
    pair = (summed * (1.0 / total_seqs) + out_bias[...]).astype(jnp.bfloat16)
    values = pair.astype(jnp.float32)
    center = jnp.mean(values, axis=-1, keepdims=True)
    shifted = values - center
    spread = jnp.mean(shifted * shifted, axis=-1, keepdims=True)
    normed = (shifted * lax.rsqrt(spread + 1e-05)).astype(jnp.bfloat16)
    gate = jnp.dot(normed, gate_weight[...], preferred_element_type=jnp.float32)
    up = jnp.dot(normed, up_weight[...], preferred_element_type=jnp.float32)
    hidden = (jax.nn.silu(gate) * up).astype(jnp.bfloat16)
    moved = (values + jnp.dot(hidden, down_weight[...], preferred_element_type=jnp.float32)).astype(jnp.bfloat16)
    moved = moved.astype(jnp.float32)
    symmetric = ((moved[:count] + moved[count:]) * 0.5).astype(jnp.bfloat16)
    packed = LANES // bins_weight.shape[0]
    weight = jnp.concatenate([bins_weight[...]] * packed, axis=0)
    bias = jnp.concatenate([bins_bias[...]] * packed, axis=1)
    logits = lax.dot_general(symmetric, weight, NT, preferred_element_type=jnp.float32) + bias
    return symmetric.astype(jnp.float32), logits


def there_kernel(total_seqs, depth_count, core_ref, chip_ref, *refs):
    params, (symmetric_out, logits_out) = refs[:-2], refs[-2:]
    summed = core_ref[...]
    if depth_count > 1:
        summed = summed + chip_ref[summed.shape[0] :, :]
    symmetric_out[...], logits_out[...] = half_row(total_seqs, summed, *params)


def here_kernel(dims, block_tiles, total_seqs, keep_ref, relay_ref, symmetric_there, logits_there, *refs):
    _, depth_count, sub_count = dims
    params, (symmetric_out, bins_out) = refs[:-2], refs[-2:]
    count, pair_channels = symmetric_there.shape
    bins = params[-2].shape[0]
    piece = count // len(block_tiles)
    band = piece * sub_count
    packed = LANES // bins
    tile, sub = lax.axis_index("tile"), lax.axis_index("sub")
    lane = lax.broadcasted_iota(jnp.int32, (1, LANES), 1)

    def write(side, symmetric, logits):
        for k, bits in enumerate(block_tiles):
            half = sub ^ (parity(bits) ^ side)
            start = (tile ^ bits) * band + half * piece
            row = k * piece
            for j in range(piece):
                at = pl.multiple_of((start + j) * pair_channels, pair_channels)
                symmetric_out[:, pl.ds(at, pair_channels)] = symmetric[row + j : row + j + 1].astype(jnp.bfloat16)
            for j in range(0, piece, packed):
                line = logits[row + j : row + j + 1]
                for p in range(1, packed):
                    line = jnp.where(lane < p * bins, line, logits[row + j + p : row + j + p + 1])
                at = pl.multiple_of((start + j) * bins, LANES)
                bins_out[:, pl.ds(at, LANES)] = line

    write(1, symmetric_there[...], logits_there[...])
    summed = keep_ref[...]
    if depth_count > 1:
        summed = summed + relay_ref[...]
    write(0, *half_row(total_seqs, summed, *params))


def call(kernel, flops, outs, scratch, operands, sources=()):
    arrays = [(a.shape, a.dtype) for a in (*operands, *outs)]
    arrays += [(a.shape, a.dtype) for a in scratch if a.memory_space == pltpu.VMEM]
    size = sum(math.prod(dims) * jnp.dtype(kind).itemsize for dims, kind in arrays)
    return pl.pallas_call(
        kernel,
        out_shape=outs,
        in_specs=[VMEM] * len(operands) + [HBM] * len(sources),
        out_specs=(VMEM,) * len(outs),
        scratch_shapes=scratch,
        compiler_params=pltpu.CompilerParams(vmem_limit_bytes=min(2 * size + (2 << 20), 60 << 20)),
        cost_estimate=pl.CostEstimate(flops=flops, bytes_accessed=size, transcendentals=0),
    )(*operands, *(pltpu.with_memory_space_constraint(s, pltpu.HBM) for s in sources))


def shape(rows, columns, kind):
    return jax.ShapeDtypeStruct((rows, columns), kind)


def per_device(
    left_mantissa,
    left_exponent,
    right_mantissa,
    right_exponent,
    residue_mask,
    out_weight,
    out_bias,
    gate_weight,
    up_weight,
    down_weight,
    distogram_weight,
    distogram_bias,
):
    tile_count, depth_count, sub_count = (lax.axis_size(a) for a in GROUP)
    seqs, width = left_mantissa.shape
    band = left_exponent.shape[1]
    piece = right_exponent.shape[1]
    channels = width // band
    fold = channels // ROWS
    residues = residue_mask.shape[0]
    pair_channels = out_weight.shape[1]
    bins = distogram_weight.shape[1]
    if channels * fold != LANES or piece * bins % LANES or sub_count != 2 or band != depth_count * sub_count or tile_count & (tile_count - 1) or band & (band - 1):
        raise ValueError("unsupported mesh")
    dims = (channels, depth_count, sub_count)
    bf16, f32 = jnp.bfloat16, jnp.float32

    sources = (left_mantissa, left_exponent.T, right_mantissa.T, right_exponent.T, residue_mask)
    (own,) = call(
        prepare_kernel,
        1 << 16,
        (shape(2 * piece * channels, seqs, bf16),),
        [pltpu.VMEM(s.shape, s.dtype) for s in sources[:4]]
        + [
            pltpu.SMEM(residue_mask.shape, residue_mask.dtype),
            pltpu.VMEM((width, seqs), bf16),
            pltpu.SemaphoreType.DMA((1,)),
        ],
        (),
        sources,
    )
    blocks = {0: own}
    for bit in bits_of(tile_count):
        for bits in list(blocks):
            blocks[bits ^ bit] = xor_permute(blocks[bits], bit, 0, 1)
    other = xor_permute(own, 0, 0, 1)
    order = list(blocks)
    early, late = order[: max(len(order) * 3 // 4, 1)], order[max(len(order) * 3 // 4, 1) :]
    count = len(order) * piece
    params = (
        out_weight,
        out_bias.reshape(1, -1),
        gate_weight,
        up_weight,
        down_weight,
        distogram_weight.T,
        distogram_bias.reshape(1, -1),
    )
    terms, left_rows, right_rows, weight, *params = call(
        functools.partial(early_kernel, dims, len(early), count),
        1 << 26,
        (
            shape(band * 2 * count, pair_channels, f32),
            shape(band * channels, seqs, bf16),
            shape(band * channels, seqs, bf16),
            *(shape(*p.shape, p.dtype) for p in params),
        ),
        [
            pltpu.VMEM((sub_count, fold, piece, ROWS, seqs), bf16),
            pltpu.VMEM((sub_count, piece, channels, seqs), bf16),
            pltpu.VMEM((2 * band * len(early) * piece * ROWS, LANES), f32),
            pltpu.SemaphoreType.DMA((2,)),
        ],
        (*(blocks[k] for k in early), other),
        params,
    )
    keep, core, chip = call(
        functools.partial(late_kernel, dims, len(late), count),
        1 << 26,
        (
            shape(2 * count, pair_channels, f32),
            shape(2 * count, pair_channels, f32),
            shape(max(band - sub_count, 1) * 2 * count, pair_channels, f32),
        ),
        [pltpu.VMEM((2 * band * len(late) * piece * ROWS, LANES), f32)],
        (*(blocks[k] for k in late), left_rows, right_rows, weight, terms),
    )
    block_tiles = tuple(order)
    size = sub_count * 2 * count
    for bit in bits_of(depth_count)[:-1]:
        rows = jnp.concatenate([keep, core, chip], axis=0)
        rows = rows.reshape(-1, 2, bit, size // sub_count * sub_count, pair_channels)[0]
        mine = rows[0] + xor_permute(rows[1], 0, bit, 0)
        mine = mine.reshape(-1, pair_channels)
        keep, core, chip = mine[: size // 2], mine[size // 2 : size], mine[size:]
    from_chip = xor_permute(chip, 0, 1, 1) if depth_count > 1 else chip
    from_core = xor_permute(core, 0, 0, 1)
    relayed = xor_permute(from_chip[: 2 * count], 0, 0, 1) if depth_count > 1 else from_core
    total_seqs = seqs * depth_count
    there = call(
        functools.partial(there_kernel, total_seqs, depth_count),
        1 << 24,
        (shape(count, pair_channels, f32), shape(count, LANES, f32)),
        [],
        (from_core, from_chip, *params),
    )
    return call(
        functools.partial(here_kernel, dims, block_tiles, total_seqs),
        1 << 24,
        (shape(1, residues * pair_channels, bf16), shape(1, residues * bins, f32)),
        [],
        (keep, relayed, *there, *params),
    )


def solution(mesh):
    in_specs = (
        P(("parts", "depth"), "tile"),
        P(("parts", "depth"), "tile"),
        P(("parts", "depth"), ("tile", "sub")),
        P(("parts", "depth"), ("tile", "sub")),
        P("parts"),
        P(),
        P(),
        P(),
        P(),
        P(),
        P(),
        P(),
    )
    out_specs = (
        P(("parts", "tile", "depth", "sub"), None),
        P(("parts", "tile", "depth", "sub"), None),
    )
    step = jax.shard_map(
        per_device, mesh=mesh, in_specs=in_specs, out_specs=out_specs, check_vma=False
    )
    known = [0]
    for bit in bits_of(mesh.shape["tile"]):
        for bits in list(known):
            known.append(bits ^ bit)
    return step
```
